128 devices in a mesh: grp: 32 (over z, y, core), tp: 4 (over x).
Axes of the slice: x: 4, y: 4, z: 4, core: 2. Of those that a mesh axis runs over, the one named last changes fastest.
Arguments:
- tokens: bfloat16 [32768, 2048], P('grp', 'tp'), may hold values from -6 to 6
- ln_gain: float32 [2048], replicated, may hold values from 0.25 to 1.75
- ln_bias: float32 [2048], replicated, may hold values from -3 to 3
- w_qkv: bfloat16 [2048, 6144], P(None, 'tp'), may hold values from -0.5 to 0.5
- b_qkv: float32 [6144], P('tp'), may hold values from -3 to 3
- w_out: bfloat16 [2048, 2048], P('tp'), may hold values from -0.125 to 0.125
- b_out: float32 [2048], P('tp'), may hold values from -3 to 3
- kv_cache: bfloat16 [65536, 4096], P('grp', 'tp'), may hold values from -24 to 24
- prefix_len: int32 [32], replicated, may hold values from 1 to 2048, as said below
- kv_pages: bfloat16 [256, 3, 128, 4096], P('grp', None, None, 'tp'), may hold values from -6 to 6
- page_table: int32 [256, 2], P('grp'), may hold values from 0 to 15, as said below
Outputs:
- mixed: bfloat16 [32768, 2048], P('grp', 'tp')
- decode_pages: bfloat16 [32, 16, 3, 128, 2048], P('grp', None, None, None, 'tp')
The draws below stay inside these ranges and needn't reach their ends.
Inputs may be any that keep to these rules, and one draw needn't show every extreme that they name: prefix_len: every group between 1 and 2048, and some group exactly 2048. page_table: column 0 a request below 16, column 1 a slot below 16; every (request, slot) pair is named by exactly one page row; the 8 rows of one group name each request once or not at all.
All inputs are finite; a program needn't handle non-finite values.
Results may differ from the reference program's by a relative error of at most 0.027.
Values may be sent and summed in bfloat16 or wider, within the bound.
A program may use at most 192 MiB of HBM per device.

```python
import jax
import jax.numpy as jnp
from jax import lax

D = 2048
HEADS = 16
HD = 128
SPAN = 1024
PREFIX = 2048
PAGES_DEV = 8
PAGE = 128
LAYERS_MOVED = 3
GROUPS = 32
TOKENS = 32768
REQUESTS = 16
SLOTS = 16
N_TP = 4


def draw_prefix_len(key, part):
    first, second = jax.random.split(jax.random.fold_in(key, 11))
    lengths = jax.random.randint(first, (GROUPS,), 1, PREFIX + 1)
    longest = jax.random.randint(second, (), 0, GROUPS)
    return jnp.where(jnp.arange(GROUPS) == longest, PREFIX, lengths).astype(jnp.int32)


def draw_page_table(key, part):
    first, second, third = jax.random.split(jax.random.fold_in(key, 23), 3)
    shuffle = jax.random.permutation(first, REQUESTS)
    inside = jax.vmap(lambda sub: jax.random.permutation(sub, PAGES_DEV))(jax.random.split(second, GROUPS))
    ranks = jnp.arange(GROUPS)[:, None] * PAGES_DEV + inside
    request_pre = ranks % REQUESTS
    arrival = ranks // REQUESTS
    orders = jax.vmap(lambda sub: jax.random.permutation(sub, SLOTS))(jax.random.split(third, REQUESTS))
    slot_ids = orders[request_pre, arrival]
    wanted = shuffle[request_pre]
    return jnp.stack([wanted.reshape(-1), slot_ids.reshape(-1)], axis=1).astype(jnp.int32)


def levels(rng, extent, cuts, least, top_value):
    level = 1.0
    for dim, shards_of in cuts:
        steps = jax.random.uniform(jax.random.fold_in(jax.random.fold_in(rng, 6), dim), (shards_of,), jnp.float32, least / len(cuts), top_value / len(cuts))
        level = level * jnp.repeat(jnp.exp(steps), extent[dim] // shards_of).reshape((-1,) + (1,) * (len(extent) - 1 - dim))
    return level


def gaussian(stream_key, dims, scale, bound, shards=(), kind=jnp.bfloat16):
    values = scale * jax.random.normal(stream_key, dims, jnp.float32)
    if shards:
        values = values * levels(stream_key, dims, shards, -0.22, 0.18)
    return jnp.clip(values, -bound, bound).astype(kind)


def setup_inputs(seed: int = 0) -> dict:
    keys = jax.random.split(jax.random.key(seed), 12)
    return {
        "tokens": gaussian(keys[0], (TOKENS, D), 1.0, 6.0, ((0, 32), (1, 4))),
        "ln_gain": jnp.clip(1.0 + 0.15 * jax.random.normal(keys[1], (D,), jnp.float32), 0.25, 1.75),
        "ln_bias": gaussian(keys[2], (D,), 0.5, 3.0, (), jnp.float32),
        "w_qkv": gaussian(keys[3], (D, 3 * D), (D // 16) ** -0.5, 0.5, ((1, 4),)),
        "b_qkv": gaussian(keys[4], (3 * D,), 0.5, 3.0, ((0, 4),), jnp.float32),
        "w_out": gaussian(keys[5], (D, D), D ** -0.5, 0.125, ((0, 4),)),
        "b_out": gaussian(keys[6], (D,), 0.5, 3.0, ((0, 4),), jnp.float32),
        "kv_cache": gaussian(keys[7], (GROUPS * PREFIX, 2 * D), 4.0, 24.0, ((0, 32), (1, 4))),
        "prefix_len": draw_prefix_len(jax.random.fold_in(keys[11], 71), 0),
        "kv_pages": gaussian(keys[9], (GROUPS * PAGES_DEV, LAYERS_MOVED, PAGE, 2 * D), 1.0, 6.0, ((0, 32), (3, 4))),
        "page_table": draw_page_table(jax.random.fold_in(keys[11], 71), 0),
    }


NEG = -1e+30
EPS = 1e-05

def reference(tokens, ln_gain, ln_bias, w_qkv, b_qkv, w_out, b_out, kv_cache, prefix_len, kv_pages, page_table):
    per_head = HEADS // N_TP

    def attend_group(inputs):
        rows, cache, length = inputs
        wide = rows.astype(jnp.float32)
        center = lax.optimization_barrier(jnp.mean(wide, axis=1, keepdims=True))
        spread = lax.optimization_barrier(jnp.mean(wide * wide, axis=1, keepdims=True)) - center * center
        normed = ((wide - center) * lax.rsqrt(spread + EPS) * ln_gain + ln_bias).astype(jnp.bfloat16)
        projected = jnp.dot(normed, w_qkv, preferred_element_type=jnp.float32) + b_qkv
        pieces = projected.reshape(SPAN, N_TP, 3, per_head, HD)
        queries = (pieces[:, :, 0] * HD ** (-0.5)).astype(jnp.bfloat16).reshape(SPAN, HEADS, HD)
        new_keys = pieces[:, :, 1].astype(jnp.bfloat16).reshape(SPAN, HEADS, HD)
        new_values = pieces[:, :, 2].astype(jnp.bfloat16).reshape(SPAN, HEADS, HD)
        stored = cache.reshape(PREFIX, N_TP, per_head, 2, HD)
        old_keys = stored[:, :, :, 0].reshape(PREFIX, HEADS, HD)
        old_values = stored[:, :, :, 1].reshape(PREFIX, HEADS, HD)
        all_keys = jnp.concatenate([old_keys, new_keys], axis=0)
        all_values = jnp.concatenate([old_values, new_values], axis=0)
        scores = jnp.einsum('chd,khd->hck', queries.astype(jnp.float32), all_keys.astype(jnp.float32))
        position = jnp.arange(PREFIX + SPAN)
        query_row = jnp.arange(SPAN)
        allowed = jnp.where(position[None, :] < PREFIX, position[None, :] < length, position[None, :] - PREFIX <= query_row[:, None])
        scores = jnp.where(allowed[None], scores, NEG)
        highest = lax.optimization_barrier(jnp.max(scores, axis=2, keepdims=True))
        expo = jnp.exp(scores - highest)
        totals = lax.optimization_barrier(jnp.sum(expo, axis=2))
        weights = expo.astype(jnp.bfloat16)
        summed = jnp.einsum('hck,khd->hcd', weights.astype(jnp.float32), all_values.astype(jnp.float32))
        attended = (summed / totals[:, :, None]).astype(jnp.bfloat16)
        return jnp.transpose(attended, (1, 0, 2)).reshape(SPAN, HEADS * HD)
    attended = lax.map(attend_group, (tokens.reshape(GROUPS, SPAN, D), kv_cache.reshape(GROUPS, PREFIX, 2 * D), prefix_len))
    mixed = (tokens.astype(jnp.float32) + jnp.dot(attended.reshape(TOKENS, D), w_out, preferred_element_type=jnp.float32) + b_out).astype(jnp.bfloat16)
    row_count = kv_pages.shape[0]
    halves = kv_pages.reshape(row_count, LAYERS_MOVED, PAGE, N_TP, 2, D // N_TP)
    wanted = page_table[:, 0].astype(jnp.int32)
    slot_ids = page_table[:, 1].astype(jnp.int32)
    decode_pages = jnp.zeros((GROUPS, SLOTS, LAYERS_MOVED, PAGE, D), jnp.bfloat16)
    for parity in range(2):
        chosen = halves[:, :, :, :, parity, :].reshape(row_count, LAYERS_MOVED, PAGE, D)
        decode_pages = decode_pages.at[2 * wanted + parity, slot_ids].set(chosen)
    return (mixed, decode_pages)
```

```python
import functools

import jax
import jax.numpy as jnp
from jax import lax
from jax.experimental import pallas as pl
from jax.experimental.pallas import tpu as pltpu
from jax.sharding import PartitionSpec as P

HEADS = 16
ROWS = 256
WIDE = 1024


NEG = -1e30
EPS = 1e-05

MESH = pl.DeviceIdType.MESH
ANY = pl.BlockSpec(memory_space=pl.ANY)
VMEM = pl.BlockSpec(memory_space=pltpu.VMEM)
SMEM = pl.BlockSpec(memory_space=pltpu.SMEM)


def swap_kernel(
    groups, table_ref, pages_ref, half_ref, tables_ref, own_sem, sent_sem, got_sem, page_out, page_in
):
    me = lax.axis_index("grp")
    core = lax.rem(me, 2)
    partner = me + 1 - 2 * core
    half_width = half_ref.shape[-1]
    page_count = pages_ref.shape[0]

    barrier = pltpu.get_barrier_semaphore()

    def greet(step, none):
        peer = lax.rem(me + step, groups)
        pl.semaphore_signal(barrier, inc=1, device_id={"grp": peer}, device_id_type=MESH)
        return none

    lax.fori_loop(1, groups, greet, 0)
    own = pltpu.make_async_copy(table_ref, tables_ref.at[me], own_sem)
    own.start()
    pl.semaphore_wait(barrier, groups - 1)

    columns = pl.ds(pl.multiple_of((1 - core) * half_width, half_width), half_width)

    def page_copy(number):
        return pltpu.make_async_remote_copy(
            src_ref=pages_ref.at[number, :, :, columns],
            dst_ref=half_ref.at[number],
            send_sem=page_out.at[number],
            recv_sem=page_in.at[number],
            device_id={"grp": partner},
            device_id_type=MESH,
        )

    def table_copy(step):
        return pltpu.make_async_remote_copy(
            src_ref=table_ref,
            dst_ref=tables_ref.at[me],
            send_sem=sent_sem.at[step],
            recv_sem=got_sem.at[step],
            device_id={"grp": lax.rem(me + step, groups)},
            device_id_type=MESH,
        )

    def start_table(step, none):
        table_copy(step).start()
        return none

    def wait_table(step, none):
        table_copy(step).wait()
        return none

    lax.fori_loop(1, groups, start_table, 0)
    for number in range(page_count):
        page_copy(number).start()
    lax.fori_loop(1, groups, wait_table, 0)
    for number in range(page_count):
        page_copy(number).wait()
    own.wait()


def swap_halves(page_table, kv_pages):
    groups = lax.axis_size("grp")
    page_count, layers, page_len, width = kv_pages.shape
    return pl.pallas_call(
        functools.partial(swap_kernel, groups),
        name="swap_halves",
        out_shape=(
            jax.ShapeDtypeStruct((page_count, layers, page_len, width // 2), kv_pages.dtype),
            jax.ShapeDtypeStruct((groups,) + page_table.shape, page_table.dtype),
        ),
        in_specs=[ANY, ANY],
        out_specs=(ANY, ANY),
        scratch_shapes=[
            pltpu.SemaphoreType.DMA,
            pltpu.SemaphoreType.DMA((groups,)),
            pltpu.SemaphoreType.DMA((groups,)),
            pltpu.SemaphoreType.DMA((page_count,)),
            pltpu.SemaphoreType.DMA((page_count,)),
        ],
        compiler_params=pltpu.CompilerParams(collective_id=1, has_side_effects=True),
    )(page_table, kv_pages)


def sort_kernel(source_ref, pages_ref, half_ref, sorted_ref, held, in_sem, out_sem):
    core = lax.rem(lax.axis_index("grp"), 2)
    half_width = half_ref.shape[-1]
    page_count = pages_ref.shape[0]
    columns = pl.ds(pl.multiple_of(core * half_width, half_width), half_width)
    count = sorted_ref.shape[0]

    for slot in range(count):
        source = source_ref[slot]

        @pl.when(source < page_count)
        def _():
            pltpu.make_async_copy(
                pages_ref.at[source, :, :, columns], held.at[slot], in_sem.at[slot]
            ).start()

        @pl.when(source >= page_count)
        def _():
            pltpu.make_async_copy(
                half_ref.at[source - page_count], held.at[slot], in_sem.at[slot]
            ).start()

    outs = []
    for slot in range(count):
        pltpu.make_async_copy(half_ref.at[0], held.at[slot], in_sem.at[slot]).wait()
        out = pltpu.make_async_copy(held.at[slot], sorted_ref.at[slot], out_sem.at[slot])
        out.start()
        outs.append(out)
    for out in outs:
        out.wait()


def sort_pages(source, kv_pages, half, count):
    shape = (count,) + half.shape[1:]
    return pl.pallas_call(
        sort_kernel,
        name="sort_pages",
        out_shape=jax.ShapeDtypeStruct(shape, half.dtype),
        in_specs=[SMEM, ANY, ANY],
        out_specs=ANY,
        scratch_shapes=[
            pltpu.VMEM(shape, half.dtype),
            pltpu.SemaphoreType.DMA((count,)),
            pltpu.SemaphoreType.DMA((count,)),
        ],
    )(source, kv_pages, half)


def place_kernel(rounds, *refs):
    slots = refs[:rounds]
    valids = refs[rounds : 2 * rounds]
    arrived = refs[2 * rounds : 3 * rounds]
    placed_ref, held, in_sem, out_sem = refs[3 * rounds :]
    count = arrived[0].shape[0]
    for number in range(rounds):
        for chip in range(count):
            pltpu.make_async_copy(
                arrived[number].at[chip], held.at[chip], in_sem.at[chip]
            ).start()
        for chip in range(count):
            pltpu.make_async_copy(
                arrived[number].at[chip], held.at[chip], in_sem.at[chip]
            ).wait()

            @pl.when(valids[number][chip] > 0)
            def _():
                pltpu.make_async_copy(
                    held.at[chip], placed_ref.at[0, slots[number][chip]], out_sem.at[chip]
                ).start()

        for chip in range(count):

            @pl.when(valids[number][chip] > 0)
            def _():
                pltpu.make_async_copy(
                    held.at[chip], placed_ref.at[0, slots[number][chip]], out_sem.at[chip]
                ).wait()


def place_pages(slots, valids, arrived):
    rounds = len(arrived)
    count = arrived[0].shape[0]
    return pl.pallas_call(
        functools.partial(place_kernel, rounds),
        name="place_pages",
        out_shape=jax.ShapeDtypeStruct((1,) + arrived[0].shape, arrived[0].dtype),
        in_specs=[SMEM] * (2 * rounds) + [ANY] * rounds,
        out_specs=ANY,
        scratch_shapes=[
            pltpu.VMEM(arrived[0].shape, arrived[0].dtype),
            pltpu.SemaphoreType.DMA((count,)),
            pltpu.SemaphoreType.DMA((count,)),
        ],
    )(*slots, *valids, *arrived)


def move_pages(kv_pages, page_table):
    groups = lax.axis_size("grp")
    chips = groups // 2
    page_count = kv_pages.shape[0]
    half, tables = swap_halves(page_table, kv_pages)
    wanted = tables[:, :, 0].reshape(chips, 2 * page_count)
    slot_ids = tables[:, :, 1].reshape(chips, 2 * page_count)
    me = lax.axis_index("grp")
    chip = me // 2
    core = me % 2
    order = jnp.arange(2 * page_count)
    again = jnp.any(
        (wanted[:, :, None] == wanted[:, None, :]) & (order[None, :, None] > order[None, None, :]),
        axis=2,
    )
    own = lax.dynamic_index_in_dim(wanted, chip, 0, keepdims=False)
    own_again = lax.dynamic_index_in_dim(again, chip, 0, keepdims=False)
    local = (order + 2 * page_count - page_count * core) % (2 * page_count)

    def source_of(number):
        fits = (own[None, :] == jnp.arange(chips)[:, None]) & (own_again == (number > 0))[None, :]
        return jnp.sum(jnp.where(fits, local[None, :], 0), axis=1).astype(jnp.int32)

    def labels_of(number):
        fits = (wanted == chip) & (again == (number > 0))
        slot = jnp.sum(jnp.where(fits, slot_ids, 0), axis=1).astype(jnp.int32)
        return slot, jnp.any(fits, axis=1).astype(jnp.int32)

    across = [list(range(0, groups, 2)), list(range(1, groups, 2))]

    def exchange(number):
        outgoing = sort_pages(source_of(number), kv_pages, half, chips)
        return lax.all_to_all(
            outgoing, "grp", split_axis=0, concat_axis=0, tiled=True, axis_index_groups=across
        )

    first = exchange(0)
    slot, valid = labels_of(0)

    def finish():
        def twice(arrived):
            second = exchange(1)
            slot2, valid2 = labels_of(1)
            return place_pages((slot, slot2), (valid, valid2), (arrived, second))

        def once(arrived):
            return place_pages((slot,), (valid,), (arrived,))

        return lax.cond(jnp.any(again), twice, once, first)

    return finish


def flash(state, queries, keys, values, allowed):
    scores = lax.dot_general(
        queries, keys, (((1,), (1,)), ((), ())), preferred_element_type=jnp.float32
    )
    if allowed is not None:
        scores = jnp.where(allowed, scores, NEG)
    top = jnp.max(scores, axis=1, keepdims=True)
    if state is None:
        raised = top
    else:
        highest, totals, running = state
        raised = jnp.maximum(highest, top)
    expo = jnp.exp(scores - raised)
    sums = jnp.sum(expo, axis=1, keepdims=True)
    part = jnp.dot(expo.astype(jnp.bfloat16), values, preferred_element_type=jnp.float32)
    if state is None:
        return raised, sums, part
    factor = jnp.exp(highest - raised)
    return raised, totals * factor + sums, running * factor + part


def block_kernel(
    tp,
    head_count,
    tokens_ref,
    gain_ref,
    bias_ref,
    w_qkv_ref,
    b_qkv_ref,
    w_out_ref,
    b_out_ref,
    cache_ref,
    length_ref,
    mixed_ref,
    whole,
    w_qkv,
    w_out,
    cache,
    normed,
    qkv,
    attended,
    terms,
    got,
    mix,
    load_sem,
    tok_out,
    tok_in,
    term_out,
    term_in,
):
    me = lax.axis_index("tp")
    rows_all, width = tokens_ref.shape
    chunks = rows_all // ROWS
    features = tp * width
    size = w_out_ref.shape[0] // head_count
    part_width = head_count * size
    prefix = cache_ref.shape[0]

    loads = [
        pltpu.make_async_copy(tokens_ref, whole.at[me], load_sem.at[0]),
        pltpu.make_async_copy(w_qkv_ref, w_qkv, load_sem.at[1]),
        pltpu.make_async_copy(cache_ref, cache, load_sem.at[2]),
        pltpu.make_async_copy(w_out_ref, w_out, load_sem.at[3]),
    ]
    for load in loads:
        load.start()

    barrier = pltpu.get_barrier_semaphore()
    for step in range(1, tp):
        pl.semaphore_signal(
            barrier, inc=1, device_id={"tp": lax.rem(me + step, tp)}, device_id_type=MESH
        )
    pl.semaphore_wait(barrier, tp - 1)

    def rows_of(chunk):
        return pl.ds(pl.multiple_of(chunk * ROWS, ROWS), ROWS)

    def token_copy(chunk, step):
        rows = rows_of(chunk)
        return pltpu.make_async_remote_copy(
            src_ref=tokens_ref.at[rows],
            dst_ref=whole.at[me, rows],
            send_sem=tok_out.at[chunk, step],
            recv_sem=tok_in.at[chunk, step],
            device_id={"tp": lax.rem(me + step, tp)},
            device_id_type=MESH,
        )

    def term_copy(chunk, step):
        rows = rows_of(chunk)
        return pltpu.make_async_remote_copy(
            src_ref=terms.at[step, rows],
            dst_ref=got.at[step, rows],
            send_sem=term_out.at[chunk, step],
            recv_sem=term_in.at[chunk, step],
            device_id={"tp": lax.rem(me + step, tp)},
            device_id_type=MESH,
        )

    order = (2, 1, 3)
    for chunk in range(chunks):
        for step in order:
            token_copy(chunk, step).start()
    for load in loads:
        load.wait()

    length = length_ref[lax.axis_index("grp")]

    def finish(chunk):
        rows = rows_of(chunk)
        total = mix[rows, :]
        for step in order:
            term_copy(chunk, step).wait_recv()
            total += got[step, rows, :].astype(jnp.float32)
        mixed_ref[rows, :] = total.astype(jnp.bfloat16)

    def visit(chunk, none):
        rows = rows_of(chunk)
        for step in order:
            token_copy(chunk, step).wait_recv()
        sums = jnp.zeros((ROWS, 1), jnp.float32)
        squares = jnp.zeros((ROWS, 1), jnp.float32)
        for peer in range(tp):
            piece = whole[peer, rows, :].astype(jnp.float32)
            sums += jnp.sum(piece, axis=1, keepdims=True)
            squares += jnp.sum(piece * piece, axis=1, keepdims=True)
        center = sums * (1.0 / features)
        spread = squares * (1.0 / features) - center * center
        scale = lax.rsqrt(spread + EPS)
        for peer in range(tp):
            columns = pl.ds(peer * width, width)
            piece = whole[peer, rows, :].astype(jnp.float32)
            normed[:, columns] = (
                (piece - center) * scale * gain_ref[:, columns] + bias_ref[:, columns]
            ).astype(jnp.bfloat16)
        for part in range(3):
            columns = pl.ds(part * part_width, part_width)
            projected = (
                jnp.dot(normed[...], w_qkv[:, columns], preferred_element_type=jnp.float32)
                + b_qkv_ref[:, columns]
            )
            if part == 0:
                projected = projected * size ** (-0.5)
            qkv[rows, columns] = projected.astype(jnp.bfloat16)

        def head(number, none):
            def lanes(start):
                return pl.ds(pl.multiple_of(start, size), size)

            queries = qkv[rows, lanes(number * size)]
            state = None
            for block in range(prefix // WIDE):
                base = block * WIDE
                keys = cache[pl.ds(base, WIDE), lanes(number * 2 * size)]
                values = cache[pl.ds(base, WIDE), lanes(number * 2 * size + size)]
                position = base + lax.broadcasted_iota(jnp.int32, (1, WIDE), 1)
                state = flash(state, queries, keys, values, position < length)

            def earlier(other, state):
                keys = qkv[rows_of(other), lanes(part_width + number * size)]
                values = qkv[rows_of(other), lanes(2 * part_width + number * size)]
                return flash(state, queries, keys, values, None)

            state = lax.fori_loop(0, chunk, earlier, state)
            keys = qkv[rows, lanes(part_width + number * size)]
            values = qkv[rows, lanes(2 * part_width + number * size)]
            causal = lax.broadcasted_iota(jnp.int32, (ROWS, ROWS), 1) <= lax.broadcasted_iota(
                jnp.int32, (ROWS, ROWS), 0
            )
            highest, totals, running = flash(state, queries, keys, values, causal)
            attended[:, lanes(number * size)] = (running / totals).astype(jnp.bfloat16)
            return none

        lax.fori_loop(0, head_count, head, 0)

        def term(step):
            columns = pl.ds(pl.multiple_of(lax.rem(me + step, tp) * width, width), width)
            return jnp.dot(attended[...], w_out[:, columns], preferred_element_type=jnp.float32)

        for step in order:
            terms[step, rows, :] = term(step).astype(jnp.bfloat16)
            term_copy(chunk, step).start()
        mix[rows, :] = term(0) + whole[me, rows, :].astype(jnp.float32) + b_out_ref[...]

        @pl.when(chunk > 0)
        def _():
            finish(chunk - 1)

        return none

    lax.fori_loop(0, chunks, visit, 0)
    finish(chunks - 1)
    for chunk in range(chunks):
        for step in order:
            token_copy(chunk, step).wait_send()
            term_copy(chunk, step).wait_send()


def block(tokens, ln_gain, ln_bias, w_qkv, b_qkv, w_out, b_out, kv_cache, prefix_len):
    tp = lax.axis_size("tp")
    rows, width = tokens.shape
    head_count = HEADS // tp
    chunks = rows // ROWS
    bf16 = jnp.bfloat16
    return pl.pallas_call(
        functools.partial(block_kernel, tp, head_count),
        name="block",
        out_shape=jax.ShapeDtypeStruct((rows, width), bf16),
        in_specs=[ANY, VMEM, VMEM, ANY, VMEM, ANY, VMEM, ANY, SMEM],
        out_specs=VMEM,
        scratch_shapes=[
            pltpu.VMEM((tp, rows, width), bf16),
            pltpu.VMEM(w_qkv.shape, bf16),
            pltpu.VMEM(w_out.shape, bf16),
            pltpu.VMEM(kv_cache.shape, bf16),
            pltpu.VMEM((ROWS, tp * width), bf16),
            pltpu.VMEM((rows, w_qkv.shape[1]), bf16),
            pltpu.VMEM((ROWS, w_out.shape[0]), bf16),
            pltpu.VMEM((tp, rows, width), bf16),
            pltpu.VMEM((tp, rows, width), bf16),
            pltpu.VMEM((rows, width), jnp.float32),
            pltpu.SemaphoreType.DMA((4,)),
            pltpu.SemaphoreType.DMA((chunks, tp)),
            pltpu.SemaphoreType.DMA((chunks, tp)),
            pltpu.SemaphoreType.DMA((chunks, tp)),
            pltpu.SemaphoreType.DMA((chunks, tp)),
        ],
        cost_estimate=pl.CostEstimate(
            flops=40_000_000_000, bytes_accessed=20_000_000, transcendentals=0
        ),
        compiler_params=pltpu.CompilerParams(
            collective_id=0, has_side_effects=True, vmem_limit_bytes=56 << 20
        ),
    )(
        tokens,
        ln_gain[None],
        ln_bias[None],
        w_qkv,
        b_qkv[None],
        w_out,
        b_out[None],
        kv_cache,
        prefix_len,
    )


def shards(
    tokens, ln_gain, ln_bias, w_qkv, b_qkv, w_out, b_out, kv_cache, prefix_len, kv_pages, page_table
):
    finish = move_pages(kv_pages, page_table)
    mixed = block(tokens, ln_gain, ln_bias, w_qkv, b_qkv, w_out, b_out, kv_cache, prefix_len)
    return (mixed, finish())


def solution(mesh):
    placed = (
        P("grp", "tp"),
        P(),
        P(),
        P(None, "tp"),
        P("tp"),
        P("tp", None),
        P("tp"),
        P("grp", "tp"),
        P(),
        P("grp", None, None, "tp"),
        P("grp", None),
    )
    return jax.shard_map(
        shards,
        mesh=mesh,
        in_specs=placed,
        out_specs=(P("grp", "tp"), P("grp", None, None, None, "tp")),
        check_vma=False,
    )
```

```python
import functools

import jax
import jax.numpy as jnp
from jax import lax
from jax.experimental import pallas as pl
from jax.experimental.pallas import tpu as pltpu
from jax.sharding import PartitionSpec as P

HEADS = 16
ROWS = 256
PAGE_ORDER = (4, 1, 12, 3, 5, 15, 7, 13, 8, 2, 9, 6, 11, 14, 10)
WIDE = 1024


NEG = -1e30
EPS = 1e-05

MESH = pl.DeviceIdType.MESH
ANY = pl.BlockSpec(memory_space=pl.ANY)
VMEM = pl.BlockSpec(memory_space=pltpu.VMEM)
SMEM = pl.BlockSpec(memory_space=pltpu.SMEM)


def swap_kernel(
    groups, table_ref, pages_ref, half_ref, tables_ref, own_sem, sent_sem, got_sem, page_out, page_in
):
    me = lax.axis_index("grp")
    core = lax.rem(me, 2)
    partner = me + 1 - 2 * core
    half_width = half_ref.shape[-1]
    page_count = pages_ref.shape[0]

    barrier = pltpu.get_barrier_semaphore()

    def greet(step, none):
        peer = lax.rem(me + step, groups)
        pl.semaphore_signal(barrier, inc=1, device_id={"grp": peer}, device_id_type=MESH)
        return none

    lax.fori_loop(1, groups, greet, 0)
    own = pltpu.make_async_copy(table_ref, tables_ref.at[me], own_sem)
    own.start()
    pl.semaphore_wait(barrier, groups - 1)

    columns = pl.ds(pl.multiple_of((1 - core) * half_width, half_width), half_width)

    def page_copy(number):
        return pltpu.make_async_remote_copy(
            src_ref=pages_ref.at[number, :, :, columns],
            dst_ref=half_ref.at[number],
            send_sem=page_out.at[number],
            recv_sem=page_in.at[number],
            device_id={"grp": partner},
            device_id_type=MESH,
        )

    def table_copy(step):
        return pltpu.make_async_remote_copy(
            src_ref=table_ref,
            dst_ref=tables_ref.at[me],
            send_sem=sent_sem.at[step],
            recv_sem=got_sem.at[step],
            device_id={"grp": lax.rem(me + step, groups)},
            device_id_type=MESH,
        )

    def start_table(step, none):
        table_copy(step).start()
        return none

    def wait_table(step, none):
        table_copy(step).wait()
        return none

    lax.fori_loop(1, groups, start_table, 0)
    for number in range(page_count):
        page_copy(number).start()
    lax.fori_loop(1, groups, wait_table, 0)
    for number in range(page_count):
        page_copy(number).wait()
    own.wait()


def swap_halves(page_table, kv_pages):
    groups = lax.axis_size("grp")
    page_count, layers, page_len, width = kv_pages.shape
    return pl.pallas_call(
        functools.partial(swap_kernel, groups),
        name="swap_halves",
        out_shape=(
            jax.ShapeDtypeStruct((page_count, layers, page_len, width // 2), kv_pages.dtype),
            jax.ShapeDtypeStruct((groups,) + page_table.shape, page_table.dtype),
        ),
        in_specs=[ANY, ANY],
        out_specs=(ANY, ANY),
        scratch_shapes=[
            pltpu.SemaphoreType.DMA,
            pltpu.SemaphoreType.DMA((groups,)),
            pltpu.SemaphoreType.DMA((groups,)),
            pltpu.SemaphoreType.DMA((page_count,)),
            pltpu.SemaphoreType.DMA((page_count,)),
        ],
        compiler_params=pltpu.CompilerParams(collective_id=1, has_side_effects=True),
    )(page_table, kv_pages)


def sort_kernel(source_ref, pages_ref, half_ref, sorted_ref, held, in_sem, out_sem):
    core = lax.rem(lax.axis_index("grp"), 2)
    half_width = half_ref.shape[-1]
    page_count = pages_ref.shape[0]
    columns = pl.ds(pl.multiple_of(core * half_width, half_width), half_width)
    count = sorted_ref.shape[0]

    for slot in range(count):
        source = source_ref[slot]

        @pl.when(source < page_count)
        def _():
            pltpu.make_async_copy(
                pages_ref.at[source, :, :, columns], held.at[slot], in_sem.at[slot]
            ).start()

        @pl.when(source >= page_count)
        def _():
            pltpu.make_async_copy(
                half_ref.at[source - page_count], held.at[slot], in_sem.at[slot]
            ).start()

    outs = []
    for slot in range(count):
        pltpu.make_async_copy(half_ref.at[0], held.at[slot], in_sem.at[slot]).wait()
        out = pltpu.make_async_copy(held.at[slot], sorted_ref.at[slot], out_sem.at[slot])
        out.start()
        outs.append(out)
    for out in outs:
        out.wait()


def sort_pages(source, kv_pages, half, count):
    shape = (count,) + half.shape[1:]
    return pl.pallas_call(
        sort_kernel,
        name="sort_pages",
        out_shape=jax.ShapeDtypeStruct(shape, half.dtype),
        in_specs=[SMEM, ANY, ANY],
        out_specs=ANY,
        scratch_shapes=[
            pltpu.VMEM(shape, half.dtype),
            pltpu.SemaphoreType.DMA((count,)),
            pltpu.SemaphoreType.DMA((count,)),
        ],
    )(source, kv_pages, half)


def place_kernel(rounds, *refs):
    slots = refs[:rounds]
    valids = refs[rounds : 2 * rounds]
    arrived = refs[2 * rounds : 3 * rounds]
    placed_ref, held, in_sem, out_sem = refs[3 * rounds :]
    count = arrived[0].shape[0]
    for number in range(rounds):
        for chip in range(count):
            pltpu.make_async_copy(
                arrived[number].at[chip], held.at[chip], in_sem.at[chip]
            ).start()
        for chip in range(count):
            pltpu.make_async_copy(
                arrived[number].at[chip], held.at[chip], in_sem.at[chip]
            ).wait()

            @pl.when(valids[number][chip] > 0)
            def _():
                pltpu.make_async_copy(
                    held.at[chip], placed_ref.at[0, slots[number][chip]], out_sem.at[chip]
                ).start()

        for chip in range(count):

            @pl.when(valids[number][chip] > 0)
            def _():
                pltpu.make_async_copy(
                    held.at[chip], placed_ref.at[0, slots[number][chip]], out_sem.at[chip]
                ).wait()


def place_pages(slots, valids, arrived):
    rounds = len(arrived)
    count = arrived[0].shape[0]
    return pl.pallas_call(
        functools.partial(place_kernel, rounds),
        name="place_pages",
        out_shape=jax.ShapeDtypeStruct((1,) + arrived[0].shape, arrived[0].dtype),
        in_specs=[SMEM] * (2 * rounds) + [ANY] * rounds,
        out_specs=ANY,
        scratch_shapes=[
            pltpu.VMEM(arrived[0].shape, arrived[0].dtype),
            pltpu.SemaphoreType.DMA((count,)),
            pltpu.SemaphoreType.DMA((count,)),
        ],
    )(*slots, *valids, *arrived)


def again_in(tables):
    chips = tables.shape[0] // 2
    wanted = tables[:, 0, :].reshape(chips, -1)
    order = jnp.arange(wanted.shape[1])
    return jnp.any(
        (wanted[:, :, None] == wanted[:, None, :]) & (order[None, :, None] > order[None, None, :]),
        axis=2,
    )


def move_twice(kv_pages, page_table):
    groups = lax.axis_size("grp")
    chips = groups // 2
    page_count = kv_pages.shape[0]
    half, tables = swap_halves(page_table.T, kv_pages)
    again = again_in(tables)
    wanted = tables[:, 0, :].reshape(chips, -1)
    slot_ids = tables[:, 1, :].reshape(chips, -1)
    me = lax.axis_index("grp")
    chip = me // 2
    core = me % 2
    order = jnp.arange(2 * page_count)
    own = lax.dynamic_index_in_dim(wanted, chip, 0, keepdims=False)
    own_again = lax.dynamic_index_in_dim(again, chip, 0, keepdims=False)
    local = (order + 2 * page_count - page_count * core) % (2 * page_count)
    across = [list(range(0, groups, 2)), list(range(1, groups, 2))]
    slots, valids, arrived = [], [], []
    for number in range(2):
        fits = (own[None, :] == jnp.arange(chips)[:, None]) & (own_again == (number > 0))[None, :]
        source = jnp.sum(jnp.where(fits, local[None, :], 0), axis=1).astype(jnp.int32)
        outgoing = sort_pages(source, kv_pages, half, chips)
        arrived.append(
            lax.all_to_all(
                outgoing, "grp", split_axis=0, concat_axis=0, tiled=True, axis_index_groups=across
            )
        )
        fits = (wanted == chip) & (again == (number > 0))
        slots.append(jnp.sum(jnp.where(fits, slot_ids, 0), axis=1).astype(jnp.int32))
        valids.append(jnp.any(fits, axis=1).astype(jnp.int32))
    return place_pages(slots, valids, arrived)


def flash(state, queries, keys, values, allowed):
    scores = lax.dot_general(
        queries, keys, (((1,), (1,)), ((), ())), preferred_element_type=jnp.float32
    )
    if allowed is not None:
        scores = jnp.where(allowed, scores, NEG)
    top = jnp.max(scores, axis=1, keepdims=True)
    if state is None:
        raised = top
    else:
        highest, totals, running = state
        raised = jnp.maximum(highest, top)
    expo = jnp.exp(scores - raised)
    sums = jnp.sum(expo, axis=1, keepdims=True)
    part = jnp.dot(expo.astype(jnp.bfloat16), values, preferred_element_type=jnp.float32)
    if state is None:
        return raised, sums, part
    factor = jnp.exp(highest - raised)
    return raised, totals * factor + sums, running * factor + part


def block_kernel(
    tp,
    groups,
    head_count,
    tokens_ref,
    gain_ref,
    bias_ref,
    w_qkv_ref,
    b_qkv_ref,
    w_out_ref,
    b_out_ref,
    cache_ref,
    length_ref,
    table_ref,
    pages_ref,
    mixed_ref,
    placed_ref,
    tables_ref,
    whole,
    w_qkv,
    w_out,
    cache,
    normed,
    qkv,
    attended,
    terms,
    got,
    mix,
    load_sem,
    tok_out,
    tok_in,
    relay_out,
    relay_in,
    far_out,
    far_in,
    near_out,
    near_in,
    pages,
    ordered,
    arrived,
    tables,
    tables_here,
    slots,
    sources,
    half_load,
    half_out,
    half_in,
    table_load,
    table_out,
    table_in,
    table_save,
    page_out,
    page_in,
    place_out,
):
    me = lax.axis_index("tp")
    group = lax.axis_index("grp")
    chip = group // 2
    core = lax.rem(group, 2)
    partner = group + 1 - 2 * core
    page_count = pages_ref.shape[0]
    layers = pages_ref.shape[1]
    half_width = placed_ref.shape[-1]
    near_columns = pl.ds(pl.multiple_of(core * half_width, half_width), half_width)
    far_columns = pl.ds(pl.multiple_of((1 - core) * half_width, half_width), half_width)
    rows_all, width = tokens_ref.shape
    chunks = rows_all // ROWS
    chips = groups // 2
    side = 4
    features = tp * width
    size = w_out_ref.shape[0] // head_count
    part_width = head_count * size
    prefix = cache_ref.shape[0]

    loads = [
        pltpu.make_async_copy(tokens_ref, whole.at[me], load_sem.at[0]),
        pltpu.make_async_copy(w_qkv_ref, w_qkv, load_sem.at[1]),
        pltpu.make_async_copy(cache_ref, cache, load_sem.at[2]),
        pltpu.make_async_copy(w_out_ref, w_out, load_sem.at[3]),
    ]
    loads += [
        pltpu.make_async_copy(
            pages_ref.at[number, :, :, near_columns],
            pages.at[core * page_count + number],
            half_load.at[number],
        )
        for number in range(page_count)
    ]
    loads.append(pltpu.make_async_copy(table_ref, tables.at[group], table_load))
    for load in loads:
        load.start()

    sides = (1, 3)
    barrier = pltpu.get_barrier_semaphore()
    for step in sides:
        pl.semaphore_signal(
            barrier, inc=1, device_id={"tp": lax.rem(me + step, tp)}, device_id_type=MESH
        )

    def greet(step, none):
        peer = lax.rem(group + step, groups)
        pl.semaphore_signal(barrier, inc=1, device_id={"grp": peer}, device_id_type=MESH)
        return none

    lax.fori_loop(1, groups, greet, 0)
    pl.semaphore_wait(barrier, groups - 1 + len(sides))

    def rows_of(chunk):
        return pl.ds(pl.multiple_of(chunk * ROWS, ROWS), ROWS)

    def half_of(chunk, step):
        start = chunk * ROWS + (0 if step == 1 else ROWS // 2)
        return pl.ds(pl.multiple_of(start, ROWS // 2), ROWS // 2)

    def send(src, dst, out_sem, in_sem, step):
        return pltpu.make_async_remote_copy(
            src_ref=src,
            dst_ref=dst,
            send_sem=out_sem,
            recv_sem=in_sem,
            device_id={"tp": lax.rem(me + step, tp)},
            device_id_type=MESH,
        )

    def own_copy(chunk, step):
        rows = rows_of(chunk)
        sems = tok_out.at[chunk, step], tok_in.at[chunk, step]
        return send(tokens_ref.at[rows], whole.at[me, rows], *sems, step)

    def relay_copy(chunk, step):
        block = whole.at[lax.rem(me + tp - step, tp), half_of(chunk, step)]
        return send(block, block, relay_out.at[chunk, step], relay_in.at[chunk, step], step)

    def far_copy(chunk, step):
        rows = half_of(chunk, step)
        sems = far_out.at[chunk, step], far_in.at[chunk, step]
        return send(terms.at[2, rows], got.at[2, rows], *sems, step)

    def near_copy(chunk, step):
        rows = rows_of(chunk)
        sems = near_out.at[chunk, step], near_in.at[chunk, step]
        return send(terms.at[step, rows], got.at[step, rows], *sems, step)

    def relay(chunk):
        for step in sides:
            own_copy(chunk, step).wait_recv()
        for step in sides:
            relay_copy(chunk, step).start()

    def pass_on(chunk):
        for step in sides:
            rows = half_of(chunk, step)
            far_copy(chunk, step).wait_recv()
            terms[step, rows, :] = (
                terms[step, rows, :].astype(jnp.float32) + got[2, rows, :].astype(jnp.float32)
            ).astype(jnp.bfloat16)
        for step in sides:
            near_copy(chunk, step).start()

    def half_copy(number):
        return pltpu.make_async_remote_copy(
            src_ref=pages_ref.at[number, :, :, far_columns],
            dst_ref=pages.at[core * page_count + number],
            send_sem=half_out.at[number],
            recv_sem=half_in.at[number],
            device_id={"grp": partner},
            device_id_type=MESH,
        )

    def table_copy(step):
        return pltpu.make_async_remote_copy(
            src_ref=table_ref,
            dst_ref=tables.at[group],
            send_sem=table_out.at[step],
            recv_sem=table_in.at[step],
            device_id={"grp": lax.rem(group + step, groups)},
            device_id_type=MESH,
        )

    def start_table(step, none):
        table_copy(step).start()
        return none

    def wait_table(step, none):
        table_copy(step).wait()
        return none

    def page_copy(step, layer):
        down, along = step // side, step % side
        target = (
            lax.rem(chip // side + down, side) * side + lax.rem(lax.rem(chip, side) + along, side)
        )
        return pltpu.make_async_remote_copy(
            src_ref=ordered.at[target, layer],
            dst_ref=arrived.at[chip, layer],
            send_sem=page_out.at[step, layer],
            recv_sem=page_in.at[step, layer],
            device_id={"grp": target * 2 + core},
            device_id_type=MESH,
        )

    def request_of(owner, entry):
        return tables_here[2 * owner + entry // page_count, 0, entry % page_count]

    def first_of(owner, request, value):
        found = 0
        for entry in reversed(range(2 * page_count)):
            found = jnp.where(request_of(owner, entry) == request, value(entry), found)
        return found

    for step in sides:
        own_copy(0, step).start()
    for number in range(page_count):
        half_copy(number).start()
    lax.fori_loop(1, groups, start_table, 0)
    relay(0)
    for step in sides:
        own_copy(1, step).start()
    for load in loads:
        load.wait()
    lax.fori_loop(1, groups, wait_table, 0)
    saves = [
        pltpu.make_async_copy(tables, tables_here, table_save.at[0]),
        pltpu.make_async_copy(tables, tables_ref, table_save.at[1]),
    ]
    for save in saves:
        save.start()
    for save in saves:
        save.wait()
    for number in range(page_count):
        half_copy(number).wait()

    def order_page(request, none):
        ordered[request] = pages[first_of(chip, request, lambda entry: entry)]
        return none

    lax.fori_loop(0, chips, order_page, 0)
    arrived[chip] = ordered[chip]
    for layer in range(layers):
        for step in PAGE_ORDER:
            page_copy(step, layer).start()

    def slot_from(owner, none):
        slots[owner] = first_of(
            owner,
            chip,
            lambda entry: tables_here[2 * owner + entry // page_count, 1, entry % page_count],
        )
        return none

    lax.fori_loop(0, chips, slot_from, 0)

    def source_to(slot, none):
        found = 0
        for owner in range(chips):
            found = jnp.where(slots[owner] == slot, owner, found)
        sources[slot] = found
        return none

    lax.fori_loop(0, chips, source_to, 0)

    length = length_ref[lax.axis_index("grp")]

    def finish(chunk):
        rows = rows_of(chunk)
        total = mix[rows, :]
        for step in sides:
            near_copy(chunk, step).wait_recv()
            total += got[step, rows, :].astype(jnp.float32)
        mixed_ref[rows, :] = total.astype(jnp.bfloat16)

    def visit(chunk, none):
        rows = rows_of(chunk)
        for step in sides:
            relay_copy(chunk, step).wait_recv()
        sums = jnp.zeros((ROWS, 1), jnp.float32)
        squares = jnp.zeros((ROWS, 1), jnp.float32)
        for peer in range(tp):
            piece = whole[peer, rows, :].astype(jnp.float32)
            sums += jnp.sum(piece, axis=1, keepdims=True)
            squares += jnp.sum(piece * piece, axis=1, keepdims=True)
        center = sums * (1.0 / features)
        spread = squares * (1.0 / features) - center * center
        scale = lax.rsqrt(spread + EPS)
        for peer in range(tp):
            columns = pl.ds(peer * width, width)
            piece = whole[peer, rows, :].astype(jnp.float32)
            normed[:, columns] = (
                (piece - center) * scale * gain_ref[:, columns] + bias_ref[:, columns]
            ).astype(jnp.bfloat16)
        for part in range(3):
            columns = pl.ds(part * part_width, part_width)
            projected = (
                jnp.dot(normed[...], w_qkv[:, columns], preferred_element_type=jnp.float32)
                + b_qkv_ref[:, columns]
            )
            if part == 0:
                projected = projected * size ** (-0.5)
            qkv[rows, columns] = projected.astype(jnp.bfloat16)

        def head(number, none):
            def lanes(start):
                return pl.ds(pl.multiple_of(start, size), size)

            @pl.when((number == 0) & (chunk + 1 < chunks))
            def _():
                relay(chunk + 1)

            @pl.when((number == 0) & (chunk > 0))
            def _():
                pass_on(chunk - 1)

            for later in range(2, chunks):

                @pl.when((chunk == 0) & (number == 2 * (later - 2)))
                def _():
                    for step in sides:
                        own_copy(later, step).start()

            queries = qkv[rows, lanes(number * size)]
            state = None
            for block in range(prefix // WIDE):
                base = block * WIDE
                keys = cache[pl.ds(base, WIDE), lanes(number * 2 * size)]
                values = cache[pl.ds(base, WIDE), lanes(number * 2 * size + size)]
                position = base + lax.broadcasted_iota(jnp.int32, (1, WIDE), 1)
                state = flash(state, queries, keys, values, position < length)

            def earlier(other, state):
                keys = qkv[rows_of(other), lanes(part_width + number * size)]
                values = qkv[rows_of(other), lanes(2 * part_width + number * size)]
                return flash(state, queries, keys, values, None)

            state = lax.fori_loop(0, chunk, earlier, state)
            keys = qkv[rows, lanes(part_width + number * size)]
            values = qkv[rows, lanes(2 * part_width + number * size)]
            causal = lax.broadcasted_iota(jnp.int32, (ROWS, ROWS), 1) <= lax.broadcasted_iota(
                jnp.int32, (ROWS, ROWS), 0
            )
            highest, totals, running = flash(state, queries, keys, values, causal)
            attended[:, lanes(number * size)] = (running / totals).astype(jnp.bfloat16)
            return none

        lax.fori_loop(0, head_count, head, 0)

        def term(step):
            columns = pl.ds(pl.multiple_of(lax.rem(me + step, tp) * width, width), width)
            return jnp.dot(attended[...], w_out[:, columns], preferred_element_type=jnp.float32)

        terms[2, rows, :] = term(2).astype(jnp.bfloat16)
        for step in sides:
            far_copy(chunk, step).start()
        for step in sides:
            terms[step, rows, :] = term(step).astype(jnp.bfloat16)
        mix[rows, :] = term(0) + whole[me, rows, :].astype(jnp.float32) + b_out_ref[...]

        @pl.when(chunk > 0)
        def _():
            finish(chunk - 1)

        return none

    lax.fori_loop(0, chunks, visit, 0)
    pass_on(chunks - 1)
    finish(chunks - 1)
    for chunk in range(chunks):
        for step in sides:
            own_copy(chunk, step).wait_send()
            relay_copy(chunk, step).wait_send()
            far_copy(chunk, step).wait_send()
            near_copy(chunk, step).wait_send()

    for layer in range(layers):
        for step in PAGE_ORDER:
            page_copy(step, layer).wait()

    def place_copy(slot):
        return pltpu.make_async_copy(pages.at[slot], placed_ref.at[0, slot], place_out.at[slot])

    def place(slot, none):
        pages[slot] = arrived[sources[slot]]
        place_copy(slot).start()
        return none

    def placed(slot, none):
        place_copy(slot).wait()
        return none

    lax.fori_loop(0, chips, place, 0)
    lax.fori_loop(0, chips, placed, 0)


def block(
    tokens, ln_gain, ln_bias, w_qkv, b_qkv, w_out, b_out, kv_cache, prefix_len, kv_pages, page_table
):
    tp = lax.axis_size("tp")
    groups = lax.axis_size("grp")
    page_count, layers, page_len, page_width = kv_pages.shape
    held = (groups // 2, layers, page_len, page_width // 2)
    rows, width = tokens.shape
    head_count = HEADS // tp
    chunks = rows // ROWS
    bf16 = jnp.bfloat16
    return pl.pallas_call(
        functools.partial(block_kernel, tp, groups, head_count),
        name="block",
        out_shape=(
            jax.ShapeDtypeStruct((rows, width), bf16),
            jax.ShapeDtypeStruct((1,) + held, bf16),
            jax.ShapeDtypeStruct((groups, 2, page_count), jnp.int32),
        ),
        in_specs=[ANY, VMEM, VMEM, ANY, VMEM, ANY, VMEM, ANY, SMEM, ANY, ANY],
        out_specs=(VMEM, ANY, ANY),
        scratch_shapes=[
            pltpu.VMEM((tp, rows, width), bf16),
            pltpu.VMEM(w_qkv.shape, bf16),
            pltpu.VMEM(w_out.shape, bf16),
            pltpu.VMEM(kv_cache.shape, bf16),
            pltpu.VMEM((ROWS, tp * width), bf16),
            pltpu.VMEM((rows, w_qkv.shape[1]), bf16),
            pltpu.VMEM((ROWS, w_out.shape[0]), bf16),
            pltpu.VMEM((tp, rows, width), bf16),
            pltpu.VMEM((tp, rows, width), bf16),
            pltpu.VMEM((rows, width), jnp.float32),
            pltpu.SemaphoreType.DMA((4,)),
        ]
        + [pltpu.SemaphoreType.DMA((chunks, tp))] * 8
        + [pltpu.VMEM(held, bf16)] * 3
        + [
            pltpu.VMEM((groups, 2, page_count), jnp.int32),
            pltpu.SMEM((groups, 2, page_count), jnp.int32),
            pltpu.SMEM((groups // 2,), jnp.int32),
            pltpu.SMEM((groups // 2,), jnp.int32),
            pltpu.SemaphoreType.DMA((page_count,)),
            pltpu.SemaphoreType.DMA((page_count,)),
            pltpu.SemaphoreType.DMA((page_count,)),
            pltpu.SemaphoreType.DMA,
            pltpu.SemaphoreType.DMA((groups,)),
            pltpu.SemaphoreType.DMA((groups,)),
            pltpu.SemaphoreType.DMA((2,)),
            pltpu.SemaphoreType.DMA((groups // 2, layers)),
            pltpu.SemaphoreType.DMA((groups // 2, layers)),
            pltpu.SemaphoreType.DMA((groups // 2,)),
        ],
        cost_estimate=pl.CostEstimate(
            flops=40_000_000_000, bytes_accessed=20_000_000, transcendentals=0
        ),
        compiler_params=pltpu.CompilerParams(
            collective_id=0, has_side_effects=True, vmem_limit_bytes=63 << 20
        ),
    )(
        tokens,
        ln_gain[None],
        ln_bias[None],
        w_qkv,
        b_qkv[None],
        w_out,
        b_out[None],
        kv_cache,
        prefix_len,
        page_table.T,
        kv_pages,
    )


def shards(
    tokens, ln_gain, ln_bias, w_qkv, b_qkv, w_out, b_out, kv_cache, prefix_len, kv_pages, page_table
):
    mixed, placed, tables = block(
        tokens,
        ln_gain,
        ln_bias,
        w_qkv,
        b_qkv,
        w_out,
        b_out,
        kv_cache,
        prefix_len,
        kv_pages,
        page_table,
    )
    decode_pages = lax.cond(
        jnp.any(again_in(tables)), lambda moved: move_twice(kv_pages, page_table), lambda moved: moved, placed
    )
    return (mixed, decode_pages)


def solution(mesh):
    placed = (
        P("grp", "tp"),
        P(),
        P(),
        P(None, "tp"),
        P("tp"),
        P("tp", None),
        P("tp"),
        P("grp", "tp"),
        P(),
        P("grp", None, None, "tp"),
        P("grp", None),
    )
    return jax.shard_map(
        shards,
        mesh=mesh,
        in_specs=placed,
        out_specs=(P("grp", "tp"), P("grp", None, None, None, "tp")),
        check_vma=False,
    )
```

```python
import functools

import jax
import jax.numpy as jnp
from jax import lax
from jax.experimental import pallas as pl
from jax.experimental.pallas import tpu as pltpu
from jax.sharding import PartitionSpec as P

HEADS = 16
ROWS = 256
PAGE_ORDER = (10, 9, 6, 11, 14, 8, 2, 5, 15, 7, 13, 4, 1, 12, 3)
WIDE = 512
TOGETHER = 4


NEG = -1e30
EPS = 1e-05

MESH = pl.DeviceIdType.MESH
ANY = pl.BlockSpec(memory_space=pl.ANY)
VMEM = pl.BlockSpec(memory_space=pltpu.VMEM)
SMEM = pl.BlockSpec(memory_space=pltpu.SMEM)


def swap_kernel(
    groups, table_ref, pages_ref, half_ref, tables_ref, own_sem, sent_sem, got_sem, page_out, page_in
):
    me = lax.axis_index("grp")
    core = lax.rem(me, 2)
    partner = me + 1 - 2 * core
    half_width = half_ref.shape[-1]
    page_count = pages_ref.shape[0]

    barrier = pltpu.get_barrier_semaphore()

    def greet(step, none):
        peer = lax.rem(me + step, groups)
        pl.semaphore_signal(barrier, inc=1, device_id={"grp": peer}, device_id_type=MESH)
        return none

    lax.fori_loop(1, groups, greet, 0)
    own = pltpu.make_async_copy(table_ref, tables_ref.at[me], own_sem)
    own.start()
    pl.semaphore_wait(barrier, groups - 1)

    columns = pl.ds(pl.multiple_of((1 - core) * half_width, half_width), half_width)

    def page_copy(number):
        return pltpu.make_async_remote_copy(
            src_ref=pages_ref.at[number, :, :, columns],
            dst_ref=half_ref.at[number],
            send_sem=page_out.at[number],
            recv_sem=page_in.at[number],
            device_id={"grp": partner},
            device_id_type=MESH,
        )

    def table_copy(step):
        return pltpu.make_async_remote_copy(
            src_ref=table_ref,
            dst_ref=tables_ref.at[me],
            send_sem=sent_sem.at[step],
            recv_sem=got_sem.at[step],
            device_id={"grp": lax.rem(me + step, groups)},
            device_id_type=MESH,
        )

    def start_table(step, none):
        table_copy(step).start()
        return none

    def wait_table(step, none):
        table_copy(step).wait()
        return none

    lax.fori_loop(1, groups, start_table, 0)
    for number in range(page_count):
        page_copy(number).start()
    lax.fori_loop(1, groups, wait_table, 0)
    for number in range(page_count):
        page_copy(number).wait()
    own.wait()


def swap_halves(page_table, kv_pages):
    groups = lax.axis_size("grp")
    page_count, layers, page_len, width = kv_pages.shape
    return pl.pallas_call(
        functools.partial(swap_kernel, groups),
        name="swap_halves",
        out_shape=(
            jax.ShapeDtypeStruct((page_count, layers, page_len, width // 2), kv_pages.dtype),
            jax.ShapeDtypeStruct((groups,) + page_table.shape, page_table.dtype),
        ),
        in_specs=[ANY, ANY],
        out_specs=(ANY, ANY),
        scratch_shapes=[
            pltpu.SemaphoreType.DMA,
            pltpu.SemaphoreType.DMA((groups,)),
            pltpu.SemaphoreType.DMA((groups,)),
            pltpu.SemaphoreType.DMA((page_count,)),
            pltpu.SemaphoreType.DMA((page_count,)),
        ],
        compiler_params=pltpu.CompilerParams(collective_id=1, has_side_effects=True),
    )(page_table, kv_pages)


def sort_kernel(source_ref, pages_ref, half_ref, sorted_ref, held, in_sem, out_sem):
    core = lax.rem(lax.axis_index("grp"), 2)
    half_width = half_ref.shape[-1]
    page_count = pages_ref.shape[0]
    columns = pl.ds(pl.multiple_of(core * half_width, half_width), half_width)
    count = sorted_ref.shape[0]

    for slot in range(count):
        source = source_ref[slot]

        @pl.when(source < page_count)
        def _():
            pltpu.make_async_copy(
                pages_ref.at[source, :, :, columns], held.at[slot], in_sem.at[slot]
            ).start()

        @pl.when(source >= page_count)
        def _():
            pltpu.make_async_copy(
                half_ref.at[source - page_count], held.at[slot], in_sem.at[slot]
            ).start()

    outs = []
    for slot in range(count):
        pltpu.make_async_copy(half_ref.at[0], held.at[slot], in_sem.at[slot]).wait()
        out = pltpu.make_async_copy(held.at[slot], sorted_ref.at[slot], out_sem.at[slot])
        out.start()
        outs.append(out)
    for out in outs:
        out.wait()


def sort_pages(source, kv_pages, half, count):
    shape = (count,) + half.shape[1:]
    return pl.pallas_call(
        sort_kernel,
        name="sort_pages",
        out_shape=jax.ShapeDtypeStruct(shape, half.dtype),
        in_specs=[SMEM, ANY, ANY],
        out_specs=ANY,
        scratch_shapes=[
            pltpu.VMEM(shape, half.dtype),
            pltpu.SemaphoreType.DMA((count,)),
            pltpu.SemaphoreType.DMA((count,)),
        ],
    )(source, kv_pages, half)


def place_kernel(rounds, *refs):
    slots = refs[:rounds]
    valids = refs[rounds : 2 * rounds]
    arrived = refs[2 * rounds : 3 * rounds]
    placed_ref, held, in_sem, out_sem = refs[3 * rounds :]
    count = arrived[0].shape[0]
    for number in range(rounds):
        for chip in range(count):
            pltpu.make_async_copy(
                arrived[number].at[chip], held.at[chip], in_sem.at[chip]
            ).start()
        for chip in range(count):
            pltpu.make_async_copy(
                arrived[number].at[chip], held.at[chip], in_sem.at[chip]
            ).wait()

            @pl.when(valids[number][chip] > 0)
            def _():
                pltpu.make_async_copy(
                    held.at[chip], placed_ref.at[0, slots[number][chip]], out_sem.at[chip]
                ).start()

        for chip in range(count):

            @pl.when(valids[number][chip] > 0)
            def _():
                pltpu.make_async_copy(
                    held.at[chip], placed_ref.at[0, slots[number][chip]], out_sem.at[chip]
                ).wait()


def place_pages(slots, valids, arrived):
    rounds = len(arrived)
    count = arrived[0].shape[0]
    return pl.pallas_call(
        functools.partial(place_kernel, rounds),
        name="place_pages",
        out_shape=jax.ShapeDtypeStruct((1,) + arrived[0].shape, arrived[0].dtype),
        in_specs=[SMEM] * (2 * rounds) + [ANY] * rounds,
        out_specs=ANY,
        scratch_shapes=[
            pltpu.VMEM(arrived[0].shape, arrived[0].dtype),
            pltpu.SemaphoreType.DMA((count,)),
            pltpu.SemaphoreType.DMA((count,)),
        ],
    )(*slots, *valids, *arrived)


def finish_kernel(
    slots, arrived, mixed_ref, placed_ref, out_ref, held, rows, in_sem, out_sem, rows_sem
):
    count = arrived.shape[0]

    def into(chip):
        return pltpu.make_async_copy(arrived.at[chip], held.at[chip], in_sem.at[chip])

    def out_of(chip):
        return pltpu.make_async_copy(held.at[chip], placed_ref.at[0, slots[chip]], out_sem.at[chip])

    for chip in range(count):
        into(chip).start()
    load = pltpu.make_async_copy(mixed_ref, rows, rows_sem.at[0])
    load.start()
    for chip in range(count):
        into(chip).wait()
        out_of(chip).start()
    load.wait()
    save = pltpu.make_async_copy(rows, out_ref, rows_sem.at[1])
    save.start()
    for chip in range(count):
        out_of(chip).wait()
    save.wait()


def place_once(slots, arrived, mixed):
    count = arrived.shape[0]
    return pl.pallas_call(
        finish_kernel,
        name="place_once",
        out_shape=(
            jax.ShapeDtypeStruct((1,) + arrived.shape, arrived.dtype),
            jax.ShapeDtypeStruct(mixed.shape, mixed.dtype),
        ),
        in_specs=[SMEM, ANY, ANY],
        out_specs=(ANY, ANY),
        scratch_shapes=[
            pltpu.VMEM(arrived.shape, arrived.dtype),
            pltpu.VMEM(mixed.shape, mixed.dtype),
            pltpu.SemaphoreType.DMA((count,)),
            pltpu.SemaphoreType.DMA((count,)),
            pltpu.SemaphoreType.DMA((2,)),
        ],
    )(slots, arrived, mixed)


def keep_kernel(rows_ref, out_ref):
    out_ref[...] = rows_ref[...]


def keep_rows(rows):
    return pl.pallas_call(
        keep_kernel,
        name="keep_rows",
        out_shape=jax.ShapeDtypeStruct(rows.shape, rows.dtype),
        in_specs=[VMEM],
        out_specs=VMEM,
    )(rows)


def again_in(tables):
    chips = tables.shape[0] // 2
    wanted = tables[:, 0, :].reshape(chips, -1)
    order = jnp.arange(wanted.shape[1])
    return jnp.any(
        (wanted[:, :, None] == wanted[:, None, :]) & (order[None, :, None] > order[None, None, :]),
        axis=2,
    )


def move_twice(kv_pages, page_table):
    groups = lax.axis_size("grp")
    chips = groups // 2
    page_count = kv_pages.shape[0]
    half, tables = swap_halves(page_table.T, kv_pages)
    again = again_in(tables)
    wanted = tables[:, 0, :].reshape(chips, -1)
    slot_ids = tables[:, 1, :].reshape(chips, -1)
    me = lax.axis_index("grp")
    chip = me // 2
    core = me % 2
    order = jnp.arange(2 * page_count)
    own = lax.dynamic_index_in_dim(wanted, chip, 0, keepdims=False)
    own_again = lax.dynamic_index_in_dim(again, chip, 0, keepdims=False)
    local = (order + 2 * page_count - page_count * core) % (2 * page_count)
    across = [list(range(0, groups, 2)), list(range(1, groups, 2))]
    slots, valids, arrived = [], [], []
    for number in range(2):
        fits = (own[None, :] == jnp.arange(chips)[:, None]) & (own_again == (number > 0))[None, :]
        source = jnp.sum(jnp.where(fits, local[None, :], 0), axis=1).astype(jnp.int32)
        outgoing = sort_pages(source, kv_pages, half, chips)
        arrived.append(
            lax.all_to_all(
                outgoing, "grp", split_axis=0, concat_axis=0, tiled=True, axis_index_groups=across
            )
        )
        fits = (wanted == chip) & (again == (number > 0))
        slots.append(jnp.sum(jnp.where(fits, slot_ids, 0), axis=1).astype(jnp.int32))
        valids.append(jnp.any(fits, axis=1).astype(jnp.int32))
    return place_pages(slots, valids, arrived)


def score(queries, keys, allowed):
    scores = lax.dot_general(
        queries, keys, (((1,), (1,)), ((), ())), preferred_element_type=jnp.float32
    )
    return scores if allowed is None else jnp.where(allowed, scores, NEG)


def update(state, scores, values):
    top = jnp.max(scores, axis=1, keepdims=True)
    raised = top if state is None else jnp.maximum(state[0], top)
    expo = jnp.exp(scores - raised)
    sums = jnp.sum(expo, axis=1, keepdims=True)
    part = jnp.dot(expo.astype(jnp.bfloat16), values, preferred_element_type=jnp.float32)
    if state is None:
        return raised, sums, part
    highest, totals, running = state
    factor = jnp.exp(highest - raised)
    return raised, totals * factor + sums, running * factor + part


def block_kernel(
    tp,
    groups,
    head_count,
    tokens_ref,
    gain_ref,
    bias_ref,
    w_qkv_ref,
    b_qkv_ref,
    w_out_ref,
    b_out_ref,
    cache_ref,
    length_ref,
    table_ref,
    pages_ref,
    mixed_ref,
    arrived,
    slots,
    twice_ref,
    whole,
    w_qkv,
    w_out,
    cache,
    normed,
    qkv,
    attended,
    terms,
    got,
    mix,
    load_sem,
    tok_out,
    tok_in,
    relay_out,
    relay_in,
    far_out,
    far_in,
    near_out,
    near_in,
    pages,
    ordered,
    tables,
    tables_here,
    powers,
    half_load,
    half_out,
    half_in,
    table_load,
    table_out,
    table_in,
    table_save,
    page_out,
    page_in,
    place_out,
):
    me = lax.axis_index("tp")
    group = lax.axis_index("grp")
    chip = group // 2
    core = lax.rem(group, 2)
    partner = group + 1 - 2 * core
    page_count = pages_ref.shape[0]
    layers = pages_ref.shape[1]
    half_width = arrived.shape[-1]
    near_columns = pl.ds(pl.multiple_of(core * half_width, half_width), half_width)
    far_columns = pl.ds(pl.multiple_of((1 - core) * half_width, half_width), half_width)
    rows_all, width = tokens_ref.shape
    chunks = rows_all // ROWS
    chips = groups // 2
    side = 4
    features = tp * width
    size = w_out_ref.shape[0] // head_count
    part_width = head_count * size
    prefix = cache_ref.shape[0]

    loads = [
        pltpu.make_async_copy(tokens_ref, whole.at[me], load_sem.at[0]),
        pltpu.make_async_copy(w_qkv_ref, w_qkv, load_sem.at[1]),
        pltpu.make_async_copy(cache_ref, cache, load_sem.at[2]),
        pltpu.make_async_copy(w_out_ref, w_out, load_sem.at[3]),
    ]
    loads += [
        pltpu.make_async_copy(
            pages_ref.at[number, :, :, near_columns],
            pages.at[core * page_count + number],
            half_load.at[number],
        )
        for number in range(page_count)
    ]
    loads.append(pltpu.make_async_copy(table_ref, tables.at[group], table_load))
    for load in loads:
        load.start()

    sides = (1, 3)
    barrier = pltpu.get_barrier_semaphore()
    for step in sides:
        pl.semaphore_signal(
            barrier, inc=1, device_id={"tp": lax.rem(me + step, tp)}, device_id_type=MESH
        )

    def greet(step, none):
        peer = lax.rem(group + step, groups)
        pl.semaphore_signal(barrier, inc=1, device_id={"grp": peer}, device_id_type=MESH)
        return none

    lax.fori_loop(1, groups, greet, 0)
    pl.semaphore_wait(barrier, groups - 1 + len(sides))

    def rows_of(chunk):
        return pl.ds(pl.multiple_of(chunk * ROWS, ROWS), ROWS)

    def half_of(chunk, step):
        start = chunk * ROWS + (0 if step == 1 else ROWS // 2)
        return pl.ds(pl.multiple_of(start, ROWS // 2), ROWS // 2)

    def send(src, dst, out_sem, in_sem, step):
        return pltpu.make_async_remote_copy(
            src_ref=src,
            dst_ref=dst,
            send_sem=out_sem,
            recv_sem=in_sem,
            device_id={"tp": lax.rem(me + step, tp)},
            device_id_type=MESH,
        )

    def own_copy(chunk, step, side):
        rows = half_of(chunk, side)
        sems = tok_out.at[chunk, step + side // 2], tok_in.at[chunk, step + side // 2]
        return send(tokens_ref.at[rows], whole.at[me, rows], *sems, step)

    def own_start(chunk):
        for turn in (0, 2):
            for step in sides:
                own_copy(chunk, step, (step + turn) % 4).start()

    def relay_copy(chunk, step):
        block = whole.at[lax.rem(me + tp - step, tp), half_of(chunk, step)]
        return send(block, block, relay_out.at[chunk, step], relay_in.at[chunk, step], step)

    def far_copy(chunk, step):
        rows = half_of(chunk, step)
        sems = far_out.at[chunk, step], far_in.at[chunk, step]
        return send(terms.at[2, rows], got.at[2, rows], *sems, step)

    def near_copy(chunk, step, side):
        rows = half_of(chunk, side)
        sems = near_out.at[chunk, step + side // 2], near_in.at[chunk, step + side // 2]
        return send(terms.at[step, rows], got.at[step, rows], *sems, step)

    def relay(chunk):
        for step in sides:
            own_copy(chunk, step, step).wait_recv()
            relay_copy(chunk, step).start()

    def pass_on(chunk):
        for step in sides:
            rows = half_of(chunk, step)
            far_copy(chunk, step).wait_recv()
            terms[step, rows, :] = (
                terms[step, rows, :].astype(jnp.float32) + got[2, rows, :].astype(jnp.float32)
            ).astype(jnp.bfloat16)
            near_copy(chunk, step, step).start()

    def half_copy(number):
        return pltpu.make_async_remote_copy(
            src_ref=pages_ref.at[number, :, :, far_columns],
            dst_ref=pages.at[core * page_count + number],
            send_sem=half_out.at[number],
            recv_sem=half_in.at[number],
            device_id={"grp": partner},
            device_id_type=MESH,
        )

    def table_copy(step):
        return pltpu.make_async_remote_copy(
            src_ref=table_ref,
            dst_ref=tables.at[group],
            send_sem=table_out.at[step],
            recv_sem=table_in.at[step],
            device_id={"grp": lax.rem(group + step, groups)},
            device_id_type=MESH,
        )

    def start_table(step, none):
        table_copy(step).start()
        return none

    def wait_table(step, none):
        table_copy(step).wait()
        return none

    piece = pages_ref.shape[2] // 2

    def page_copy(step, part):
        layer, lines = part // 2, pl.ds(part % 2 * piece, piece)
        down, along = step // side, step % side
        target = (
            lax.rem(chip // side + down, side) * side + lax.rem(lax.rem(chip, side) + along, side)
        )
        return pltpu.make_async_remote_copy(
            src_ref=ordered.at[target, layer, lines],
            dst_ref=arrived.at[chip, layer, lines],
            send_sem=page_out.at[step, part],
            recv_sem=page_in.at[step, part],
            device_id={"grp": target * 2 + core},
            device_id_type=MESH,
        )

    def request_of(owner, entry):
        return tables_here[2 * owner + entry // page_count, 0, entry % page_count]

    def first_of(owner, request, value):
        found = 0
        for entry in reversed(range(2 * page_count)):
            found = jnp.where(request_of(owner, entry) == request, value(entry), found)
        return found

    own_start(0)
    for number in range(page_count):
        half_copy(number).start()
    lax.fori_loop(1, groups, start_table, 0)
    relay(0)
    own_start(1)
    for load in loads:
        load.wait()
    lax.fori_loop(1, groups, wait_table, 0)
    save = pltpu.make_async_copy(tables, tables_here, table_save)
    save.start()
    save.wait()
    for number in range(page_count):
        half_copy(number).wait()

    def order_page(request, none):
        ordered[request] = pages[first_of(chip, request, lambda entry: entry)]
        return none

    lax.fori_loop(0, chips, order_page, 0)
    stay = pltpu.make_async_copy(ordered.at[chip], arrived.at[chip], place_out)
    stay.start()
    for part in range(2 * layers):
        for step in PAGE_ORDER:
            page_copy(step, part).start()

    def slot_from(owner, none):
        slots[owner] = first_of(
            owner,
            chip,
            lambda entry: tables_here[2 * owner + entry // page_count, 1, entry % page_count],
        )
        return none

    lax.fori_loop(0, chips, slot_from, 0)

    for request in range(chips):
        powers[request] = 1 << request

    def repeats(owner, twice):
        total = 0
        for entry in range(2 * page_count):
            total += powers[request_of(owner, entry)]
        return jnp.where(total == (1 << chips) - 1, twice, 1)

    twice_ref[0] = lax.fori_loop(0, chips, repeats, 0)

    length = length_ref[lax.axis_index("grp")]

    def finish(chunk):
        rows = rows_of(chunk)
        total = mix[rows, :]
        for step in sides:
            for side in sides:
                near_copy(chunk, step, side).wait_recv()
            total += got[step, rows, :].astype(jnp.float32)
        mixed_ref[rows, :] = total.astype(jnp.bfloat16)

    def visit(chunk, none):
        rows = rows_of(chunk)
        for step in sides:
            own_copy(chunk, step, 4 - step).wait_recv()
            relay_copy(chunk, step).wait_recv()
        sums = jnp.zeros((ROWS, 1), jnp.float32)
        squares = jnp.zeros((ROWS, 1), jnp.float32)
        for peer in range(tp):
            piece = whole[peer, rows, :].astype(jnp.float32)
            sums += jnp.sum(piece, axis=1, keepdims=True)
            squares += jnp.sum(piece * piece, axis=1, keepdims=True)
        center = sums * (1.0 / features)
        spread = squares * (1.0 / features) - center * center
        scale = lax.rsqrt(spread + EPS)
        for peer in range(tp):
            columns = pl.ds(peer * width, width)
            piece = whole[peer, rows, :].astype(jnp.float32)
            normed[:, columns] = (
                (piece - center) * scale * gain_ref[:, columns] + bias_ref[:, columns]
            ).astype(jnp.bfloat16)
        for part in range(3):
            columns = pl.ds(part * part_width, part_width)
            projected = (
                jnp.dot(normed[...], w_qkv[:, columns], preferred_element_type=jnp.float32)
                + b_qkv_ref[columns][None, :]
            )
            if part == 0:
                projected = projected * size ** (-0.5)
            qkv[rows, columns] = projected.astype(jnp.bfloat16)

        @pl.when(chunk + 1 < chunks)
        def _():
            relay(chunk + 1)

        for later in range(2, chunks):

            @pl.when(chunk == later - 2)
            def _():
                own_start(later)

        def head(number, none):
            def lanes(start):
                return pl.ds(pl.multiple_of(start, size), size)

            heads = [number * TOGETHER + other for other in range(TOGETHER)]
            queries = [qkv[rows, lanes(at * size)] for at in heads]

            def new_block(states, other, allowed):
                scores = [
                    score(query, qkv[rows_of(other), lanes(part_width + at * size)], allowed)
                    for query, at in zip(queries, heads)
                ]
                return tuple(
                    update(state, each, qkv[rows_of(other), lanes(2 * part_width + at * size)])
                    for state, each, at in zip(states, scores, heads)
                )

            states = (None,) * TOGETHER
            for block in range(prefix // WIDE):
                base = pl.ds(block * WIDE, WIDE)
                position = block * WIDE + lax.broadcasted_iota(jnp.int32, (1, WIDE), 1)
                scores = [
                    score(query, cache[base, lanes(at * 2 * size)], position < length)
                    for query, at in zip(queries, heads)
                ]
                states = tuple(
                    update(state, each, cache[base, lanes(at * 2 * size + size)])
                    for state, each, at in zip(states, scores, heads)
                )
            states = lax.fori_loop(
                0, chunk, lambda other, states: new_block(states, other, None), states
            )
            causal = lax.broadcasted_iota(jnp.int32, (ROWS, ROWS), 1) <= lax.broadcasted_iota(
                jnp.int32, (ROWS, ROWS), 0
            )
            states = new_block(states, chunk, causal)
            for (highest, totals, running), at in zip(states, heads):
                attended[:, lanes(at * size)] = (running / totals).astype(jnp.bfloat16)
            return none

        lax.fori_loop(0, head_count // TOGETHER, head, 0)

        @pl.when(chunk > 0)
        def _():
            pass_on(chunk - 1)

        @pl.when(chunk > 1)
        def _():
            finish(chunk - 2)

        def term(step):
            columns = pl.ds(pl.multiple_of(lax.rem(me + step, tp) * width, width), width)
            return jnp.dot(attended[...], w_out[:, columns], preferred_element_type=jnp.float32)

        terms[2, rows, :] = term(2).astype(jnp.bfloat16)
        for step in sides:
            far_copy(chunk, step).start()
        for step in sides:
            terms[step, rows, :] = term(step).astype(jnp.bfloat16)
            near_copy(chunk, step, 4 - step).start()
        mix[rows, :] = term(0) + whole[me, rows, :].astype(jnp.float32) + b_out_ref[...]

        return none

    lax.fori_loop(0, chunks, visit, 0)
    finish(chunks - 2)
    pass_on(chunks - 1)
    finish(chunks - 1)
    for chunk in range(chunks):
        for step in sides:
            for side in sides:
                own_copy(chunk, step, side).wait_send()
                near_copy(chunk, step, side).wait_send()
            relay_copy(chunk, step).wait_send()
            far_copy(chunk, step).wait_send()

    for part in range(2 * layers):
        for step in PAGE_ORDER:
            page_copy(step, part).wait()

    stay.wait()


def block(
    tokens, ln_gain, ln_bias, w_qkv, b_qkv, w_out, b_out, kv_cache, prefix_len, kv_pages, page_table
):
    tp = lax.axis_size("tp")
    groups = lax.axis_size("grp")
    page_count, layers, page_len, page_width = kv_pages.shape
    held = (groups // 2, layers, page_len, page_width // 2)
    rows, width = tokens.shape
    head_count = HEADS // tp
    chunks = rows // ROWS
    bf16 = jnp.bfloat16
    return pl.pallas_call(
        functools.partial(block_kernel, tp, groups, head_count),
        name="block",
        out_shape=(
            jax.ShapeDtypeStruct((rows, width), bf16),
            jax.ShapeDtypeStruct(held, bf16),
            jax.ShapeDtypeStruct((groups // 2,), jnp.int32),
            jax.ShapeDtypeStruct((1,), jnp.int32),
        ),
        in_specs=[ANY, VMEM, VMEM, ANY, VMEM, ANY, VMEM, ANY, SMEM, ANY, ANY],
        out_specs=(VMEM, ANY, SMEM, SMEM),
        scratch_shapes=[
            pltpu.VMEM((tp, rows, width), bf16),
            pltpu.VMEM(w_qkv.shape, bf16),
            pltpu.VMEM(w_out.shape, bf16),
            pltpu.VMEM(kv_cache.shape, bf16),
            pltpu.VMEM((ROWS, tp * width), bf16),
            pltpu.VMEM((rows, w_qkv.shape[1]), bf16),
            pltpu.VMEM((ROWS, w_out.shape[0]), bf16),
            pltpu.VMEM((tp, rows, width), bf16),
            pltpu.VMEM((tp, rows, width), bf16),
            pltpu.VMEM((rows, width), jnp.float32),
            pltpu.SemaphoreType.DMA((4,)),
        ]
        + [pltpu.SemaphoreType.DMA((chunks, tp + 2))] * 8
        + [pltpu.VMEM(held, bf16)] * 2
        + [
            pltpu.VMEM((groups, 2, page_count), jnp.int32),
            pltpu.SMEM((groups, 2, page_count), jnp.int32),
            pltpu.SMEM((groups // 2,), jnp.int32),
            pltpu.SemaphoreType.DMA((page_count,)),
            pltpu.SemaphoreType.DMA((page_count,)),
            pltpu.SemaphoreType.DMA((page_count,)),
            pltpu.SemaphoreType.DMA,
            pltpu.SemaphoreType.DMA((groups,)),
            pltpu.SemaphoreType.DMA((groups,)),
            pltpu.SemaphoreType.DMA,
            pltpu.SemaphoreType.DMA((groups // 2, 2 * layers)),
            pltpu.SemaphoreType.DMA((groups // 2, 2 * layers)),
            pltpu.SemaphoreType.DMA,
        ],
        cost_estimate=pl.CostEstimate(
            flops=40_000_000_000, bytes_accessed=20_000_000, transcendentals=0
        ),
        compiler_params=pltpu.CompilerParams(
            collective_id=0, has_side_effects=True, vmem_limit_bytes=63 << 20
        ),
    )(
        tokens,
        ln_gain[None],
        ln_bias[None],
        w_qkv,
        b_qkv,
        w_out,
        b_out[None],
        kv_cache,
        prefix_len,
        page_table.T,
        kv_pages,
    )


def shards(
    tokens, ln_gain, ln_bias, w_qkv, b_qkv, w_out, b_out, kv_cache, prefix_len, kv_pages, page_table
):
    mixed, arrived, slots, twice = block(
        tokens,
        ln_gain,
        ln_bias,
        w_qkv,
        b_qkv,
        w_out,
        b_out,
        kv_cache,
        prefix_len,
        kv_pages,
        page_table,
    )
    decode_pages, mixed = lax.cond(
        twice[0] > 0,
        lambda *once: (move_twice(kv_pages, page_table), keep_rows(once[2])),
        place_once,
        slots,
        arrived,
        mixed,
    )
    return (mixed, decode_pages)


def solution(mesh):
    placed = (
        P("grp", "tp"),
        P(),
        P(),
        P(None, "tp"),
        P("tp"),
        P("tp", None),
        P("tp"),
        P("grp", "tp"),
        P(),
        P("grp", None, None, "tp"),
        P("grp", None),
    )
    return jax.shard_map(
        shards,
        mesh=mesh,
        in_specs=placed,
        out_specs=(P("grp", "tp"), P("grp", None, None, None, "tp")),
        check_vma=False,
    )
```

```python
import functools

import jax
import jax.numpy as jnp
from jax import lax
from jax.experimental import pallas as pl
from jax.experimental.pallas import tpu as pltpu
from jax.sharding import PartitionSpec as P

HEADS = 16
ROWS = 256
PARTS = 6
PAGE_ORDER = (10, 9, 6, 11, 14, 8, 2, 5, 15, 7, 13, 4, 1, 12, 3)
WIDE = 512
TOGETHER = 4


NEG = -1e30
EPS = 1e-05

MESH = pl.DeviceIdType.MESH
ANY = pl.BlockSpec(memory_space=pl.ANY)
VMEM = pl.BlockSpec(memory_space=pltpu.VMEM)
SMEM = pl.BlockSpec(memory_space=pltpu.SMEM)


def swap_kernel(
    groups, table_ref, pages_ref, half_ref, tables_ref, own_sem, sent_sem, got_sem, page_out, page_in
):
    me = lax.axis_index("grp")
    core = lax.rem(me, 2)
    partner = me + 1 - 2 * core
    half_width = half_ref.shape[-1]
    page_count = pages_ref.shape[0]

    barrier = pltpu.get_barrier_semaphore()

    def greet(step, none):
        peer = lax.rem(me + step, groups)
        pl.semaphore_signal(barrier, inc=1, device_id={"grp": peer}, device_id_type=MESH)
        return none

    lax.fori_loop(1, groups, greet, 0)
    own = pltpu.make_async_copy(table_ref, tables_ref.at[me], own_sem)
    own.start()
    pl.semaphore_wait(barrier, groups - 1)

    columns = pl.ds(pl.multiple_of((1 - core) * half_width, half_width), half_width)

    def page_copy(number):
        return pltpu.make_async_remote_copy(
            src_ref=pages_ref.at[number, :, :, columns],
            dst_ref=half_ref.at[number],
            send_sem=page_out.at[number],
            recv_sem=page_in.at[number],
            device_id={"grp": partner},
            device_id_type=MESH,
        )

    def table_copy(step):
        return pltpu.make_async_remote_copy(
            src_ref=table_ref,
            dst_ref=tables_ref.at[me],
            send_sem=sent_sem.at[step],
            recv_sem=got_sem.at[step],
            device_id={"grp": lax.rem(me + step, groups)},
            device_id_type=MESH,
        )

    def start_table(step, none):
        table_copy(step).start()
        return none

    def wait_table(step, none):
        table_copy(step).wait()
        return none

    lax.fori_loop(1, groups, start_table, 0)
    for number in range(page_count):
        page_copy(number).start()
    lax.fori_loop(1, groups, wait_table, 0)
    for number in range(page_count):
        page_copy(number).wait()
    own.wait()


def swap_halves(page_table, kv_pages):
    groups = lax.axis_size("grp")
    page_count, layers, page_len, width = kv_pages.shape
    return pl.pallas_call(
        functools.partial(swap_kernel, groups),
        name="swap_halves",
        out_shape=(
            jax.ShapeDtypeStruct((page_count, layers, page_len, width // 2), kv_pages.dtype),
            jax.ShapeDtypeStruct((groups,) + page_table.shape, page_table.dtype),
        ),
        in_specs=[ANY, ANY],
        out_specs=(ANY, ANY),
        scratch_shapes=[
            pltpu.SemaphoreType.DMA,
            pltpu.SemaphoreType.DMA((groups,)),
            pltpu.SemaphoreType.DMA((groups,)),
            pltpu.SemaphoreType.DMA((page_count,)),
            pltpu.SemaphoreType.DMA((page_count,)),
        ],
        compiler_params=pltpu.CompilerParams(collective_id=1, has_side_effects=True),
    )(page_table, kv_pages)


def sort_kernel(source_ref, pages_ref, half_ref, sorted_ref, held, in_sem, out_sem):
    core = lax.rem(lax.axis_index("grp"), 2)
    half_width = half_ref.shape[-1]
    page_count = pages_ref.shape[0]
    columns = pl.ds(pl.multiple_of(core * half_width, half_width), half_width)
    count = sorted_ref.shape[0]

    for slot in range(count):
        source = source_ref[slot]

        @pl.when(source < page_count)
        def _():
            pltpu.make_async_copy(
                pages_ref.at[source, :, :, columns], held.at[slot], in_sem.at[slot]
            ).start()

        @pl.when(source >= page_count)
        def _():
            pltpu.make_async_copy(
                half_ref.at[source - page_count], held.at[slot], in_sem.at[slot]
            ).start()

    outs = []
    for slot in range(count):
        pltpu.make_async_copy(half_ref.at[0], held.at[slot], in_sem.at[slot]).wait()
        out = pltpu.make_async_copy(held.at[slot], sorted_ref.at[slot], out_sem.at[slot])
        out.start()
        outs.append(out)
    for out in outs:
        out.wait()


def sort_pages(source, kv_pages, half, count):
    shape = (count,) + half.shape[1:]
    return pl.pallas_call(
        sort_kernel,
        name="sort_pages",
        out_shape=jax.ShapeDtypeStruct(shape, half.dtype),
        in_specs=[SMEM, ANY, ANY],
        out_specs=ANY,
        scratch_shapes=[
            pltpu.VMEM(shape, half.dtype),
            pltpu.SemaphoreType.DMA((count,)),
            pltpu.SemaphoreType.DMA((count,)),
        ],
    )(source, kv_pages, half)


def place_kernel(rounds, *refs):
    slots = refs[:rounds]
    valids = refs[rounds : 2 * rounds]
    arrived = refs[2 * rounds : 3 * rounds]
    placed_ref, held, in_sem, out_sem = refs[3 * rounds :]
    count = arrived[0].shape[0]
    for number in range(rounds):
        for chip in range(count):
            pltpu.make_async_copy(
                arrived[number].at[chip], held.at[chip], in_sem.at[chip]
            ).start()
        for chip in range(count):
            pltpu.make_async_copy(
                arrived[number].at[chip], held.at[chip], in_sem.at[chip]
            ).wait()

            @pl.when(valids[number][chip] > 0)
            def _():
                pltpu.make_async_copy(
                    held.at[chip], placed_ref.at[0, slots[number][chip]], out_sem.at[chip]
                ).start()

        for chip in range(count):

            @pl.when(valids[number][chip] > 0)
            def _():
                pltpu.make_async_copy(
                    held.at[chip], placed_ref.at[0, slots[number][chip]], out_sem.at[chip]
                ).wait()


def place_pages(slots, valids, arrived):
    rounds = len(arrived)
    count = arrived[0].shape[0]
    return pl.pallas_call(
        functools.partial(place_kernel, rounds),
        name="place_pages",
        out_shape=jax.ShapeDtypeStruct((1,) + arrived[0].shape, arrived[0].dtype),
        in_specs=[SMEM] * (2 * rounds) + [ANY] * rounds,
        out_specs=ANY,
        scratch_shapes=[
            pltpu.VMEM(arrived[0].shape, arrived[0].dtype),
            pltpu.SemaphoreType.DMA((count,)),
            pltpu.SemaphoreType.DMA((count,)),
        ],
    )(*slots, *valids, *arrived)


def finish_kernel(
    slots, arrived, mixed_ref, placed_ref, out_ref, held, rows, in_sem, out_sem, rows_sem
):
    count = arrived.shape[0]

    def into(chip):
        return pltpu.make_async_copy(arrived.at[chip], held.at[chip], in_sem.at[chip])

    def out_of(chip):
        return pltpu.make_async_copy(held.at[chip], placed_ref.at[0, slots[chip]], out_sem.at[chip])

    for chip in range(count):
        into(chip).start()
    load = pltpu.make_async_copy(mixed_ref, rows, rows_sem.at[0])
    load.start()
    for chip in range(count):
        into(chip).wait()
        out_of(chip).start()
    load.wait()
    save = pltpu.make_async_copy(rows, out_ref, rows_sem.at[1])
    save.start()
    for chip in range(count):
        out_of(chip).wait()
    save.wait()


def place_once(slots, arrived, mixed):
    count = arrived.shape[0]
    return pl.pallas_call(
        finish_kernel,
        name="place_once",
        out_shape=(
            jax.ShapeDtypeStruct((1,) + arrived.shape, arrived.dtype),
            jax.ShapeDtypeStruct(mixed.shape, mixed.dtype),
        ),
        in_specs=[SMEM, ANY, ANY],
        out_specs=(ANY, pl.BlockSpec(memory_space=pltpu.HBM)),
        scratch_shapes=[
            pltpu.VMEM(arrived.shape, arrived.dtype),
            pltpu.VMEM(mixed.shape, mixed.dtype),
            pltpu.SemaphoreType.DMA((count,)),
            pltpu.SemaphoreType.DMA((count,)),
            pltpu.SemaphoreType.DMA((2,)),
        ],
    )(slots, arrived, mixed)


def keep_kernel(rows_ref, out_ref):
    pltpu.sync_copy(rows_ref, out_ref)


def keep_rows(rows):
    return pl.pallas_call(
        keep_kernel,
        name="keep_rows",
        out_shape=jax.ShapeDtypeStruct(rows.shape, rows.dtype),
        in_specs=[VMEM],
        out_specs=pl.BlockSpec(memory_space=pltpu.HBM),
    )(rows)


def again_in(tables):
    chips = tables.shape[0] // 2
    wanted = tables[:, 0, :].reshape(chips, -1)
    order = jnp.arange(wanted.shape[1])
    return jnp.any(
        (wanted[:, :, None] == wanted[:, None, :]) & (order[None, :, None] > order[None, None, :]),
        axis=2,
    )


def move_twice(kv_pages, page_table):
    groups = lax.axis_size("grp")
    chips = groups // 2
    page_count = kv_pages.shape[0]
    half, tables = swap_halves(page_table.T, kv_pages)
    again = again_in(tables)
    wanted = tables[:, 0, :].reshape(chips, -1)
    slot_ids = tables[:, 1, :].reshape(chips, -1)
    me = lax.axis_index("grp")
    chip = me // 2
    core = me % 2
    order = jnp.arange(2 * page_count)
    own = lax.dynamic_index_in_dim(wanted, chip, 0, keepdims=False)
    own_again = lax.dynamic_index_in_dim(again, chip, 0, keepdims=False)
    local = (order + 2 * page_count - page_count * core) % (2 * page_count)
    across = [list(range(0, groups, 2)), list(range(1, groups, 2))]
    slots, valids, arrived = [], [], []
    for number in range(2):
        fits = (own[None, :] == jnp.arange(chips)[:, None]) & (own_again == (number > 0))[None, :]
        source = jnp.sum(jnp.where(fits, local[None, :], 0), axis=1).astype(jnp.int32)
        outgoing = sort_pages(source, kv_pages, half, chips)
        arrived.append(
            lax.all_to_all(
                outgoing, "grp", split_axis=0, concat_axis=0, tiled=True, axis_index_groups=across
            )
        )
        fits = (wanted == chip) & (again == (number > 0))
        slots.append(jnp.sum(jnp.where(fits, slot_ids, 0), axis=1).astype(jnp.int32))
        valids.append(jnp.any(fits, axis=1).astype(jnp.int32))
    return place_pages(slots, valids, arrived)


def score(queries, keys, allowed):
    scores = lax.dot_general(
        queries, keys, (((1,), (1,)), ((), ())), preferred_element_type=jnp.float32
    )
    return scores if allowed is None else jnp.where(allowed, scores, NEG)


def update(state, scores, values):
    top = jnp.max(scores, axis=1, keepdims=True)
    raised = top if state is None else jnp.maximum(state[0], top)
    expo = jnp.exp(scores - raised)
    sums = jnp.sum(expo, axis=1, keepdims=True)
    part = jnp.dot(expo.astype(jnp.bfloat16), values, preferred_element_type=jnp.float32)
    if state is None:
        return raised, sums, part
    highest, totals, running = state
    factor = jnp.exp(highest - raised)
    return raised, totals * factor + sums, running * factor + part


def block_kernel(
    tp,
    groups,
    head_count,
    tokens_ref,
    gain_ref,
    bias_ref,
    w_qkv_ref,
    b_qkv_ref,
    w_out_ref,
    b_out_ref,
    cache_ref,
    length_ref,
    table_ref,
    pages_ref,
    mixed_ref,
    arrived,
    slots,
    twice_ref,
    whole,
    w_qkv,
    w_out,
    cache,
    normed,
    qkv,
    attended,
    terms,
    got,
    mix,
    load_sem,
    tok_out,
    tok_in,
    relay_out,
    relay_in,
    far_out,
    far_in,
    near_out,
    near_in,
    ordered,
    tables,
    tables_here,
    powers,
    picks,
    half_load,
    half_out,
    half_in,
    table_load,
    table_out,
    table_in,
    table_save,
    page_out,
    page_in,
    place_out,
    *pages,
):
    me = lax.axis_index("tp")
    group = lax.axis_index("grp")
    chip = group // 2
    core = lax.rem(group, 2)
    partner = group + 1 - 2 * core
    page_count = pages_ref.shape[0]
    layers = pages_ref.shape[1]
    half_width = arrived.shape[-1]
    near_columns = pl.ds(pl.multiple_of(core * half_width, half_width), half_width)
    far_columns = pl.ds(pl.multiple_of((1 - core) * half_width, half_width), half_width)
    rows_all, width = tokens_ref.shape
    chunks = rows_all // ROWS
    chips = groups // 2
    side = 4
    features = tp * width
    size = w_out_ref.shape[0] // head_count
    part_width = head_count * size
    prefix = cache_ref.shape[0]

    loads = [
        pltpu.make_async_copy(tokens_ref, whole.at[me], load_sem.at[0]),
        pltpu.make_async_copy(w_qkv_ref, w_qkv, load_sem.at[1]),
        pltpu.make_async_copy(cache_ref, cache, load_sem.at[2]),
        pltpu.make_async_copy(w_out_ref, w_out, load_sem.at[3]),
    ]
    parts = len(pages)
    piece = pages_ref.shape[2] * layers // parts
    ours = pl.ds(pl.multiple_of(core * page_count, page_count), page_count)

    def place_of(part):
        layer, line = divmod(part * piece, pages_ref.shape[2])
        return layer, pl.ds(line, piece)

    def piece_load(part):
        return pltpu.make_async_copy(
            pages_ref.at[:, *place_of(part), near_columns], pages[part].at[ours], half_load.at[part]
        )

    table_own = pltpu.make_async_copy(table_ref, tables.at[group], table_load)
    table_own.start()
    for part in range(parts):
        piece_load(part).start()
    for load in loads:
        load.start()

    sides = (1, 3)
    barrier = pltpu.get_barrier_semaphore()
    for step in sides:
        pl.semaphore_signal(
            barrier, inc=1, device_id={"tp": lax.rem(me + step, tp)}, device_id_type=MESH
        )

    def greet(step, none):
        peer = lax.rem(group + step, groups)
        pl.semaphore_signal(barrier, inc=1, device_id={"grp": peer}, device_id_type=MESH)
        return none

    lax.fori_loop(1, groups, greet, 0)
    pl.semaphore_wait(barrier, groups - 1 + len(sides))

    def rows_of(chunk):
        return pl.ds(pl.multiple_of(chunk * ROWS, ROWS), ROWS)

    def half_of(chunk, step):
        start = chunk * ROWS + (0 if step == 1 else ROWS // 2)
        return pl.ds(pl.multiple_of(start, ROWS // 2), ROWS // 2)

    def send(src, dst, out_sem, in_sem, step):
        return pltpu.make_async_remote_copy(
            src_ref=src,
            dst_ref=dst,
            send_sem=out_sem,
            recv_sem=in_sem,
            device_id={"tp": lax.rem(me + step, tp)},
            device_id_type=MESH,
        )

    def own_copy(chunk, step, side):
        rows = half_of(chunk, side)
        sems = tok_out.at[chunk, step + side // 2], tok_in.at[chunk, step + side // 2]
        return send(tokens_ref.at[rows], whole.at[me, rows], *sems, step)

    def own_start(chunk):
        for turn in (0, 2):
            for step in sides:
                own_copy(chunk, step, (step + turn) % 4).start()

    def relay_copy(chunk, step):
        block = whole.at[lax.rem(me + tp - step, tp), half_of(chunk, step)]
        return send(block, block, relay_out.at[chunk, step], relay_in.at[chunk, step], step)

    def far_copy(chunk, step):
        rows = half_of(chunk, step)
        sems = far_out.at[chunk, step], far_in.at[chunk, step]
        return send(terms.at[2, rows], got.at[2, rows], *sems, step)

    def near_copy(chunk, step, side):
        rows = half_of(chunk, side)
        sems = near_out.at[chunk, step + side // 2], near_in.at[chunk, step + side // 2]
        return send(terms.at[step, rows], got.at[step, rows], *sems, step)

    def relay(chunk):
        for step in sides:
            own_copy(chunk, step, step).wait_recv()
            relay_copy(chunk, step).start()

    def pass_on(chunk):
        for step in sides:
            rows = half_of(chunk, step)
            far_copy(chunk, step).wait_recv()
            terms[step, rows, :] = (
                terms[step, rows, :].astype(jnp.float32) + got[2, rows, :].astype(jnp.float32)
            ).astype(jnp.bfloat16)
            near_copy(chunk, step, step).start()

    def half_copy(part):
        return pltpu.make_async_remote_copy(
            src_ref=pages_ref.at[:, *place_of(part), far_columns],
            dst_ref=pages[part].at[ours],
            send_sem=half_out.at[part],
            recv_sem=half_in.at[part],
            device_id={"grp": partner},
            device_id_type=MESH,
        )

    def table_copy(step):
        return pltpu.make_async_remote_copy(
            src_ref=table_ref,
            dst_ref=tables.at[group],
            send_sem=table_out.at[step],
            recv_sem=table_in.at[step],
            device_id={"grp": lax.rem(group + step, groups)},
            device_id_type=MESH,
        )

    def start_table(step, none):
        table_copy(step).start()
        return none

    def wait_table(step, none):
        table_copy(step).wait()
        return none

    def page_copy(step, part):
        down, along = step // side, step % side
        target = (
            lax.rem(chip // side + down, side) * side + lax.rem(lax.rem(chip, side) + along, side)
        )
        return pltpu.make_async_remote_copy(
            src_ref=ordered.at[target, *place_of(part)],
            dst_ref=arrived.at[chip, *place_of(part)],
            send_sem=page_out.at[step, part],
            recv_sem=page_in.at[step, part],
            device_id={"grp": target * 2 + core},
            device_id_type=MESH,
        )

    def request_of(owner, entry):
        return tables_here[2 * owner + entry // page_count, 0, entry % page_count]

    def first_of(owner, request, value):
        found = 0
        for entry in reversed(range(2 * page_count)):
            found = jnp.where(request_of(owner, entry) == request, value(entry), found)
        return found

    own_start(0)
    for part in range(parts):
        half_copy(part).start()
    lax.fori_loop(1, groups, start_table, 0)
    relay(0)
    own_start(1)
    own_start(2)
    table_own.wait()
    lax.fori_loop(1, groups, wait_table, 0)
    save = pltpu.make_async_copy(tables, tables_here, table_save)
    save.start()
    save.wait()

    def pick(request, none):
        picks[request] = first_of(chip, request, lambda entry: entry)
        return none

    lax.fori_loop(0, chips, pick, 0)

    def send_pieces(part):
        for step in PAGE_ORDER:
            page_copy(step, part).start()

    for part in range(parts):
        piece_load(part).wait()
        half_copy(part).wait_recv()
        layer, lines = place_of(part)

        def order_piece(request, none):
            ordered[request, layer, lines] = pages[part][picks[request]]
            return none

        lax.fori_loop(0, chips, order_piece, 0)
        if part:
            send_pieces(part - 1)
    send_pieces(parts - 1)
    stay = pltpu.make_async_copy(ordered.at[chip], arrived.at[chip], place_out)
    stay.start()
    for load in loads:
        load.wait()

    def slot_from(owner, none):
        slots[owner] = first_of(
            owner,
            chip,
            lambda entry: tables_here[2 * owner + entry // page_count, 1, entry % page_count],
        )
        return none

    lax.fori_loop(0, chips, slot_from, 0)

    for request in range(chips):
        powers[request] = 1 << request

    def repeats(owner, twice):
        total = 0
        for entry in range(2 * page_count):
            total += powers[request_of(owner, entry)]
        return jnp.where(total == (1 << chips) - 1, twice, 1)

    twice_ref[0] = lax.fori_loop(0, chips, repeats, 0)

    length = length_ref[lax.axis_index("grp")]

    def finish(chunk):
        rows = rows_of(chunk)
        total = mix[rows, :]
        for step in sides:
            for side in sides:
                near_copy(chunk, step, side).wait_recv()
            total += got[step, rows, :].astype(jnp.float32)
        mixed_ref[rows, :] = total.astype(jnp.bfloat16)

    def visit(chunk, none):
        @pl.when(chunk + 1 < chunks)
        def _():
            relay(chunk + 1)

        for later in range(3, chunks):

            @pl.when(chunk == later - 3)
            def _():
                own_start(later)

        rows = rows_of(chunk)
        for step in sides:
            own_copy(chunk, step, 4 - step).wait_recv()
            relay_copy(chunk, step).wait_recv()
        sums = jnp.zeros((ROWS, 1), jnp.float32)
        squares = jnp.zeros((ROWS, 1), jnp.float32)
        for peer in range(tp):
            piece = whole[peer, rows, :].astype(jnp.float32)
            sums += jnp.sum(piece, axis=1, keepdims=True)
            squares += jnp.sum(piece * piece, axis=1, keepdims=True)
        center = sums * (1.0 / features)
        spread = squares * (1.0 / features) - center * center
        scale = lax.rsqrt(spread + EPS)
        for peer in range(tp):
            columns = pl.ds(peer * width, width)
            piece = whole[peer, rows, :].astype(jnp.float32)
            normed[:, columns] = (
                (piece - center) * scale * gain_ref[:, columns] + bias_ref[:, columns]
            ).astype(jnp.bfloat16)
        for part in range(3):
            columns = pl.ds(part * part_width, part_width)
            projected = (
                jnp.dot(normed[...], w_qkv[:, columns], preferred_element_type=jnp.float32)
                + b_qkv_ref[columns][None, :]
            )
            if part == 0:
                projected = projected * size ** (-0.5)
            qkv[rows, columns] = projected.astype(jnp.bfloat16)

        def head(number, none):
            def lanes(start):
                return pl.ds(pl.multiple_of(start, size), size)

            heads = [number * TOGETHER + other for other in range(TOGETHER)]
            queries = [qkv[rows, lanes(at * size)] for at in heads]

            def new_block(states, other, allowed):
                scores = [
                    score(query, qkv[rows_of(other), lanes(part_width + at * size)], allowed)
                    for query, at in zip(queries, heads)
                ]
                return tuple(
                    update(state, each, qkv[rows_of(other), lanes(2 * part_width + at * size)])
                    for state, each, at in zip(states, scores, heads)
                )

            states = (None,) * TOGETHER
            for block in range(prefix // WIDE):
                base = pl.ds(block * WIDE, WIDE)
                position = block * WIDE + lax.broadcasted_iota(jnp.int32, (1, WIDE), 1)
                scores = [
                    score(query, cache[base, lanes(at * 2 * size)], position < length)
                    for query, at in zip(queries, heads)
                ]
                states = tuple(
                    update(state, each, cache[base, lanes(at * 2 * size + size)])
                    for state, each, at in zip(states, scores, heads)
                )
            states = lax.fori_loop(
                0, chunk, lambda other, states: new_block(states, other, None), states
            )
            causal = lax.broadcasted_iota(jnp.int32, (ROWS, ROWS), 1) <= lax.broadcasted_iota(
                jnp.int32, (ROWS, ROWS), 0
            )
            states = new_block(states, chunk, causal)
            for (highest, totals, running), at in zip(states, heads):
                attended[:, lanes(at * size)] = (running / totals).astype(jnp.bfloat16)
            return none

        lax.fori_loop(0, head_count // TOGETHER, head, 0)

        @pl.when(chunk > 0)
        def _():
            pass_on(chunk - 1)

        @pl.when(chunk > 1)
        def _():
            finish(chunk - 2)

        def term(step):
            columns = pl.ds(pl.multiple_of(lax.rem(me + step, tp) * width, width), width)
            return jnp.dot(attended[...], w_out[:, columns], preferred_element_type=jnp.float32)

        terms[2, rows, :] = term(2).astype(jnp.bfloat16)
        for step in sides:
            far_copy(chunk, step).start()
        for step in sides:
            terms[step, rows, :] = term(step).astype(jnp.bfloat16)
            near_copy(chunk, step, 4 - step).start()
        mix[rows, :] = term(0) + whole[me, rows, :].astype(jnp.float32) + b_out_ref[...]

        return none

    lax.fori_loop(0, chunks, visit, 0)
    finish(chunks - 2)
    pass_on(chunks - 1)
    finish(chunks - 1)
    for chunk in range(chunks):
        for step in sides:
            for side in sides:
                own_copy(chunk, step, side).wait_send()
                near_copy(chunk, step, side).wait_send()
            relay_copy(chunk, step).wait_send()
            far_copy(chunk, step).wait_send()

    for part in range(parts):
        half_copy(part).wait_send()
        for step in PAGE_ORDER:
            page_copy(step, part).wait()

    stay.wait()


def block(
    tokens, ln_gain, ln_bias, w_qkv, b_qkv, w_out, b_out, kv_cache, prefix_len, kv_pages, page_table
):
    tp = lax.axis_size("tp")
    groups = lax.axis_size("grp")
    page_count, layers, page_len, page_width = kv_pages.shape
    held = (groups // 2, layers, page_len, page_width // 2)
    rows, width = tokens.shape
    head_count = HEADS // tp
    chunks = rows // ROWS
    bf16 = jnp.bfloat16
    return pl.pallas_call(
        functools.partial(block_kernel, tp, groups, head_count),
        name="block",
        out_shape=(
            jax.ShapeDtypeStruct((rows, width), bf16),
            jax.ShapeDtypeStruct(held, bf16),
            jax.ShapeDtypeStruct((groups // 2,), jnp.int32),
            jax.ShapeDtypeStruct((1,), jnp.int32),
        ),
        in_specs=[ANY, VMEM, VMEM, ANY, VMEM, ANY, VMEM, ANY, SMEM, ANY, ANY],
        out_specs=(VMEM, ANY, SMEM, SMEM),
        scratch_shapes=[
            pltpu.VMEM((tp, rows, width), bf16),
            pltpu.VMEM(w_qkv.shape, bf16),
            pltpu.VMEM(w_out.shape, bf16),
            pltpu.VMEM(kv_cache.shape, bf16),
            pltpu.VMEM((ROWS, tp * width), bf16),
            pltpu.VMEM((rows, w_qkv.shape[1]), bf16),
            pltpu.VMEM((ROWS, w_out.shape[0]), bf16),
            pltpu.VMEM((tp, rows, width), bf16),
            pltpu.VMEM((tp, rows, width), bf16),
            pltpu.VMEM((rows, width), jnp.float32),
            pltpu.SemaphoreType.DMA((4,)),
        ]
        + [pltpu.SemaphoreType.DMA((chunks, tp + 2))] * 8
        + [
            pltpu.VMEM(held, bf16),
            pltpu.VMEM((groups, 2, page_count), jnp.int32),
            pltpu.SMEM((groups, 2, page_count), jnp.int32),
            pltpu.SMEM((groups // 2,), jnp.int32),
            pltpu.SMEM((groups // 2,), jnp.int32),
            pltpu.SemaphoreType.DMA((PARTS,)),
            pltpu.SemaphoreType.DMA((PARTS,)),
            pltpu.SemaphoreType.DMA((PARTS,)),
            pltpu.SemaphoreType.DMA,
            pltpu.SemaphoreType.DMA((groups,)),
            pltpu.SemaphoreType.DMA((groups,)),
            pltpu.SemaphoreType.DMA,
            pltpu.SemaphoreType.DMA((groups // 2, PARTS)),
            pltpu.SemaphoreType.DMA((groups // 2, PARTS)),
            pltpu.SemaphoreType.DMA,
        ]
        + [pltpu.VMEM((held[0], layers * page_len // PARTS, held[3]), bf16)] * PARTS,
        cost_estimate=pl.CostEstimate(
            flops=40_000_000_000, bytes_accessed=20_000_000, transcendentals=0
        ),
        compiler_params=pltpu.CompilerParams(
            collective_id=0, has_side_effects=True, vmem_limit_bytes=63 << 20
        ),
    )(
        tokens,
        ln_gain[None],
        ln_bias[None],
        w_qkv,
        b_qkv,
        w_out,
        b_out[None],
        kv_cache,
        prefix_len,
        page_table.T,
        kv_pages,
    )


def shards(
    tokens, ln_gain, ln_bias, w_qkv, b_qkv, w_out, b_out, kv_cache, prefix_len, kv_pages, page_table
):
    mixed, arrived, slots, twice = block(
        tokens,
        ln_gain,
        ln_bias,
        w_qkv,
        b_qkv,
        w_out,
        b_out,
        kv_cache,
        prefix_len,
        kv_pages,
        page_table,
    )
    decode_pages, mixed = lax.cond(
        twice[0] > 0,
        lambda *once: (move_twice(kv_pages, page_table), keep_rows(once[2])),
        place_once,
        slots,
        arrived,
        mixed,
    )
    return (mixed, decode_pages)


def solution(mesh):
    placed = (
        P("grp", "tp"),
        P(),
        P(),
        P(None, "tp"),
        P("tp"),
        P("tp", None),
        P("tp"),
        P("grp", "tp"),
        P(),
        P("grp", None, None, "tp"),
        P("grp", None),
    )
    return jax.shard_map(
        shards,
        mesh=mesh,
        in_specs=placed,
        out_specs=(P("grp", "tp"), P("grp", None, None, None, "tp")),
        check_vma=False,
    )
```

```python
import functools

import jax
import jax.numpy as jnp
from jax import lax
from jax.experimental import pallas as pl
from jax.experimental.pallas import tpu as pltpu
from jax.sharding import PartitionSpec as P

HEADS = 16
ROWS = 256
PARTS = 6
PAGE_ORDER = (10, 9, 6, 11, 14, 8, 2, 5, 15, 7, 13, 4, 1, 12, 3)
WIDE = 512
TOGETHER = 4


NEG = -1e30
EPS = 1e-05

MESH = pl.DeviceIdType.MESH
ANY = pl.BlockSpec(memory_space=pl.ANY)
VMEM = pl.BlockSpec(memory_space=pltpu.VMEM)
SMEM = pl.BlockSpec(memory_space=pltpu.SMEM)


def swap_kernel(
    groups, table_ref, pages_ref, half_ref, tables_ref, own_sem, sent_sem, got_sem, page_out, page_in
):
    me = lax.axis_index("grp")
    core = lax.rem(me, 2)
    partner = me + 1 - 2 * core
    half_width = half_ref.shape[-1]
    page_count = pages_ref.shape[0]

    barrier = pltpu.get_barrier_semaphore()

    def greet(step, none):
        peer = lax.rem(me + step, groups)
        pl.semaphore_signal(barrier, inc=1, device_id={"grp": peer}, device_id_type=MESH)
        return none

    lax.fori_loop(1, groups, greet, 0)
    own = pltpu.make_async_copy(table_ref, tables_ref.at[me], own_sem)
    own.start()
    pl.semaphore_wait(barrier, groups - 1)

    columns = pl.ds(pl.multiple_of((1 - core) * half_width, half_width), half_width)

    def page_copy(number):
        return pltpu.make_async_remote_copy(
            src_ref=pages_ref.at[number, :, :, columns],
            dst_ref=half_ref.at[number],
            send_sem=page_out.at[number],
            recv_sem=page_in.at[number],
            device_id={"grp": partner},
            device_id_type=MESH,
        )

    def table_copy(step):
        return pltpu.make_async_remote_copy(
            src_ref=table_ref,
            dst_ref=tables_ref.at[me],
            send_sem=sent_sem.at[step],
            recv_sem=got_sem.at[step],
            device_id={"grp": lax.rem(me + step, groups)},
            device_id_type=MESH,
        )

    def start_table(step, none):
        table_copy(step).start()
        return none

    def wait_table(step, none):
        table_copy(step).wait()
        return none

    lax.fori_loop(1, groups, start_table, 0)
    for number in range(page_count):
        page_copy(number).start()
    lax.fori_loop(1, groups, wait_table, 0)
    for number in range(page_count):
        page_copy(number).wait()
    own.wait()


def swap_halves(page_table, kv_pages):
    groups = lax.axis_size("grp")
    page_count, layers, page_len, width = kv_pages.shape
    return pl.pallas_call(
        functools.partial(swap_kernel, groups),
        name="swap_halves",
        out_shape=(
            jax.ShapeDtypeStruct((page_count, layers, page_len, width // 2), kv_pages.dtype),
            jax.ShapeDtypeStruct((groups,) + page_table.shape, page_table.dtype),
        ),
        in_specs=[ANY, ANY],
        out_specs=(ANY, ANY),
        scratch_shapes=[
            pltpu.SemaphoreType.DMA,
            pltpu.SemaphoreType.DMA((groups,)),
            pltpu.SemaphoreType.DMA((groups,)),
            pltpu.SemaphoreType.DMA((page_count,)),
            pltpu.SemaphoreType.DMA((page_count,)),
        ],
        compiler_params=pltpu.CompilerParams(collective_id=1, has_side_effects=True),
    )(page_table, kv_pages)


def sort_kernel(source_ref, pages_ref, half_ref, sorted_ref, held, in_sem, out_sem):
    core = lax.rem(lax.axis_index("grp"), 2)
    half_width = half_ref.shape[-1]
    page_count = pages_ref.shape[0]
    columns = pl.ds(pl.multiple_of(core * half_width, half_width), half_width)
    count = sorted_ref.shape[0]

    for slot in range(count):
        source = source_ref[slot]

        @pl.when(source < page_count)
        def _():
            pltpu.make_async_copy(
                pages_ref.at[source, :, :, columns], held.at[slot], in_sem.at[slot]
            ).start()

        @pl.when(source >= page_count)
        def _():
            pltpu.make_async_copy(
                half_ref.at[source - page_count], held.at[slot], in_sem.at[slot]
            ).start()

    outs = []
    for slot in range(count):
        pltpu.make_async_copy(half_ref.at[0], held.at[slot], in_sem.at[slot]).wait()
        out = pltpu.make_async_copy(held.at[slot], sorted_ref.at[slot], out_sem.at[slot])
        out.start()
        outs.append(out)
    for out in outs:
        out.wait()


def sort_pages(source, kv_pages, half, count):
    shape = (count,) + half.shape[1:]
    return pl.pallas_call(
        sort_kernel,
        name="sort_pages",
        out_shape=jax.ShapeDtypeStruct(shape, half.dtype),
        in_specs=[SMEM, ANY, ANY],
        out_specs=ANY,
        scratch_shapes=[
            pltpu.VMEM(shape, half.dtype),
            pltpu.SemaphoreType.DMA((count,)),
            pltpu.SemaphoreType.DMA((count,)),
        ],
    )(source, kv_pages, half)


def place_kernel(rounds, *refs):
    slots = refs[:rounds]
    valids = refs[rounds : 2 * rounds]
    arrived = refs[2 * rounds : 3 * rounds]
    placed_ref, held, in_sem, out_sem = refs[3 * rounds :]
    count = arrived[0].shape[0]
    for number in range(rounds):
        for chip in range(count):
            pltpu.make_async_copy(
                arrived[number].at[chip], held.at[chip], in_sem.at[chip]
            ).start()
        for chip in range(count):
            pltpu.make_async_copy(
                arrived[number].at[chip], held.at[chip], in_sem.at[chip]
            ).wait()

            @pl.when(valids[number][chip] > 0)
            def _():
                pltpu.make_async_copy(
                    held.at[chip], placed_ref.at[0, slots[number][chip]], out_sem.at[chip]
                ).start()

        for chip in range(count):

            @pl.when(valids[number][chip] > 0)
            def _():
                pltpu.make_async_copy(
                    held.at[chip], placed_ref.at[0, slots[number][chip]], out_sem.at[chip]
                ).wait()


def place_pages(slots, valids, arrived):
    rounds = len(arrived)
    count = arrived[0].shape[0]
    return pl.pallas_call(
        functools.partial(place_kernel, rounds),
        name="place_pages",
        out_shape=jax.ShapeDtypeStruct((1,) + arrived[0].shape, arrived[0].dtype),
        in_specs=[SMEM] * (2 * rounds) + [ANY] * rounds,
        out_specs=ANY,
        scratch_shapes=[
            pltpu.VMEM(arrived[0].shape, arrived[0].dtype),
            pltpu.SemaphoreType.DMA((count,)),
            pltpu.SemaphoreType.DMA((count,)),
        ],
    )(*slots, *valids, *arrived)


def finish_kernel(
    slots, arrived, mixed_ref, placed_ref, out_ref, held, rows, in_sem, out_sem, rows_sem
):
    count = arrived.shape[0]

    pieces = [(chip, layer) for chip in range(count) for layer in range(arrived.shape[1])]

    def into(chip, layer):
        return pltpu.make_async_copy(
            arrived.at[chip, layer], held.at[chip, layer], in_sem.at[chip, layer]
        )

    def out_of(chip, layer):
        return pltpu.make_async_copy(
            held.at[chip, layer], placed_ref.at[0, slots[chip], layer], out_sem.at[chip, layer]
        )

    for each in pieces:
        into(*each).start()
    load = pltpu.make_async_copy(mixed_ref, rows, rows_sem.at[0])
    load.start()
    for each in pieces:
        into(*each).wait()
        out_of(*each).start()
    load.wait()
    save = pltpu.make_async_copy(rows, out_ref, rows_sem.at[1])
    save.start()
    for each in pieces:
        out_of(*each).wait()
    save.wait()


def place_once(slots, arrived, mixed):
    count = arrived.shape[0]
    return pl.pallas_call(
        finish_kernel,
        name="place_once",
        out_shape=(
            jax.ShapeDtypeStruct((1,) + arrived.shape, arrived.dtype),
            jax.ShapeDtypeStruct(mixed.shape, mixed.dtype),
        ),
        in_specs=[SMEM, ANY, ANY],
        out_specs=(ANY, pl.BlockSpec(memory_space=pltpu.HBM)),
        scratch_shapes=[
            pltpu.VMEM(arrived.shape, arrived.dtype),
            pltpu.VMEM(mixed.shape, mixed.dtype),
            pltpu.SemaphoreType.DMA(arrived.shape[:2]),
            pltpu.SemaphoreType.DMA(arrived.shape[:2]),
            pltpu.SemaphoreType.DMA((2,)),
        ],
        compiler_params=pltpu.CompilerParams(vmem_limit_bytes=63 << 20),
    )(slots, arrived, mixed)


def keep_kernel(rows_ref, out_ref):
    pltpu.sync_copy(rows_ref, out_ref)


def keep_rows(rows):
    return pl.pallas_call(
        keep_kernel,
        name="keep_rows",
        out_shape=jax.ShapeDtypeStruct(rows.shape, rows.dtype),
        in_specs=[VMEM],
        out_specs=pl.BlockSpec(memory_space=pltpu.HBM),
        compiler_params=pltpu.CompilerParams(vmem_limit_bytes=63 << 20),
    )(rows)


def again_in(tables):
    chips = tables.shape[0] // 2
    wanted = tables[:, 0, :].reshape(chips, -1)
    order = jnp.arange(wanted.shape[1])
    return jnp.any(
        (wanted[:, :, None] == wanted[:, None, :]) & (order[None, :, None] > order[None, None, :]),
        axis=2,
    )


def move_twice(kv_pages, page_table):
    groups = lax.axis_size("grp")
    chips = groups // 2
    page_count = kv_pages.shape[0]
    half, tables = swap_halves(page_table.T, kv_pages)
    again = again_in(tables)
    wanted = tables[:, 0, :].reshape(chips, -1)
    slot_ids = tables[:, 1, :].reshape(chips, -1)
    me = lax.axis_index("grp")
    chip = me // 2
    core = me % 2
    order = jnp.arange(2 * page_count)
    own = lax.dynamic_index_in_dim(wanted, chip, 0, keepdims=False)
    own_again = lax.dynamic_index_in_dim(again, chip, 0, keepdims=False)
    local = (order + 2 * page_count - page_count * core) % (2 * page_count)
    across = [list(range(0, groups, 2)), list(range(1, groups, 2))]
    slots, valids, arrived = [], [], []
    for number in range(2):
        fits = (own[None, :] == jnp.arange(chips)[:, None]) & (own_again == (number > 0))[None, :]
        source = jnp.sum(jnp.where(fits, local[None, :], 0), axis=1).astype(jnp.int32)
        outgoing = sort_pages(source, kv_pages, half, chips)
        arrived.append(
            lax.all_to_all(
                outgoing, "grp", split_axis=0, concat_axis=0, tiled=True, axis_index_groups=across
            )
        )
        fits = (wanted == chip) & (again == (number > 0))
        slots.append(jnp.sum(jnp.where(fits, slot_ids, 0), axis=1).astype(jnp.int32))
        valids.append(jnp.any(fits, axis=1).astype(jnp.int32))
    return place_pages(slots, valids, arrived)


def score(queries, keys, allowed):
    scores = lax.dot_general(
        queries, keys, (((1,), (1,)), ((), ())), preferred_element_type=jnp.float32
    )
    return scores if allowed is None else jnp.where(allowed, scores, NEG)


def update(state, scores, values):
    top = jnp.max(scores, axis=1, keepdims=True)
    raised = top if state is None else jnp.maximum(state[0], top)
    expo = jnp.exp(scores - raised)
    sums = jnp.sum(expo, axis=1, keepdims=True)
    part = jnp.dot(expo.astype(jnp.bfloat16), values, preferred_element_type=jnp.float32)
    if state is None:
        return raised, sums, part
    highest, totals, running = state
    factor = jnp.exp(highest - raised)
    return raised, totals * factor + sums, running * factor + part


def block_kernel(
    tp,
    groups,
    head_count,
    tokens_ref,
    gain_ref,
    bias_ref,
    w_qkv_ref,
    b_qkv_ref,
    w_out_ref,
    b_out_ref,
    cache_ref,
    length_ref,
    table_ref,
    pages_ref,
    mixed_ref,
    arrived,
    slots,
    twice_ref,
    whole,
    w_qkv,
    w_out,
    cache,
    normed,
    qkv,
    attended,
    terms,
    got,
    mix,
    load_sem,
    tok_out,
    tok_in,
    relay_out,
    relay_in,
    far_out,
    far_in,
    near_out,
    near_in,
    ordered,
    tables,
    tables_here,
    powers,
    picks,
    half_load,
    half_out,
    half_in,
    table_load,
    table_out,
    table_in,
    table_save,
    page_out,
    page_in,
    place_out,
    *pages,
):
    me = lax.axis_index("tp")
    group = lax.axis_index("grp")
    chip = group // 2
    core = lax.rem(group, 2)
    partner = group + 1 - 2 * core
    page_count = pages_ref.shape[0]
    layers = pages_ref.shape[1]
    half_width = arrived.shape[-1]
    near_columns = pl.ds(pl.multiple_of(core * half_width, half_width), half_width)
    far_columns = pl.ds(pl.multiple_of((1 - core) * half_width, half_width), half_width)
    rows_all, width = tokens_ref.shape
    chunks = rows_all // ROWS
    chips = groups // 2
    side = 4
    features = tp * width
    size = w_out_ref.shape[0] // head_count
    part_width = head_count * size
    prefix = cache_ref.shape[0]

    loads = [
        pltpu.make_async_copy(tokens_ref, whole.at[me], load_sem.at[0]),
        pltpu.make_async_copy(w_qkv_ref, w_qkv, load_sem.at[1]),
        pltpu.make_async_copy(cache_ref, cache, load_sem.at[2]),
        pltpu.make_async_copy(w_out_ref, w_out, load_sem.at[3]),
    ]
    parts = len(pages)
    piece = pages_ref.shape[2] * layers // parts
    ours = pl.ds(pl.multiple_of(core * page_count, page_count), page_count)

    def place_of(part):
        layer, line = divmod(part * piece, pages_ref.shape[2])
        return layer, pl.ds(line, piece)

    def piece_load(part):
        return pltpu.make_async_copy(
            pages_ref.at[:, *place_of(part), near_columns], pages[part].at[ours], half_load.at[part]
        )

    table_own = pltpu.make_async_copy(table_ref, tables.at[group], table_load)
    table_own.start()
    for part in range(parts):
        piece_load(part).start()
    for load in loads:
        load.start()

    sides = (1, 3)
    barrier = pltpu.get_barrier_semaphore()
    for step in sides:
        pl.semaphore_signal(
            barrier, inc=1, device_id={"tp": lax.rem(me + step, tp)}, device_id_type=MESH
        )

    def greet(step, none):
        peer = lax.rem(group + step, groups)
        pl.semaphore_signal(barrier, inc=1, device_id={"grp": peer}, device_id_type=MESH)
        return none

    lax.fori_loop(1, groups, greet, 0)
    pl.semaphore_wait(barrier, groups - 1 + len(sides))

    def rows_of(chunk):
        return pl.ds(pl.multiple_of(chunk * ROWS, ROWS), ROWS)

    def half_of(chunk, step):
        start = chunk * ROWS + (0 if step == 1 else ROWS // 2)
        return pl.ds(pl.multiple_of(start, ROWS // 2), ROWS // 2)

    def send(src, dst, out_sem, in_sem, step):
        return pltpu.make_async_remote_copy(
            src_ref=src,
            dst_ref=dst,
            send_sem=out_sem,
            recv_sem=in_sem,
            device_id={"tp": lax.rem(me + step, tp)},
            device_id_type=MESH,
        )

    def own_copy(chunk, step, side):
        rows = half_of(chunk, side)
        sems = tok_out.at[chunk, step + side // 2], tok_in.at[chunk, step + side // 2]
        return send(tokens_ref.at[rows], whole.at[me, rows], *sems, step)

    def own_start(chunk):
        for turn in (0, 2):
            for step in sides:
                own_copy(chunk, step, (step + turn) % 4).start()

    def relay_copy(chunk, step):
        block = whole.at[lax.rem(me + tp - step, tp), half_of(chunk, step)]
        return send(block, block, relay_out.at[chunk, step], relay_in.at[chunk, step], step)

    def far_copy(chunk, step):
        rows = half_of(chunk, step)
        sems = far_out.at[chunk, step], far_in.at[chunk, step]
        return send(terms.at[2, rows], got.at[2, rows], *sems, step)

    def near_copy(chunk, step, side):
        rows = half_of(chunk, side)
        sems = near_out.at[chunk, step + side // 2], near_in.at[chunk, step + side // 2]
        return send(terms.at[step, rows], got.at[step, rows], *sems, step)

    def relay(chunk):
        for step in sides:
            own_copy(chunk, step, step).wait_recv()
            relay_copy(chunk, step).start()

    def pass_on(chunk):
        for step in sides:
            rows = half_of(chunk, step)
            far_copy(chunk, step).wait_recv()
            terms[step, rows, :] = (
                terms[step, rows, :].astype(jnp.float32) + got[2, rows, :].astype(jnp.float32)
            ).astype(jnp.bfloat16)
            near_copy(chunk, step, step).start()

    def half_copy(part):
        return pltpu.make_async_remote_copy(
            src_ref=pages_ref.at[:, *place_of(part), far_columns],
            dst_ref=pages[part].at[ours],
            send_sem=half_out.at[part],
            recv_sem=half_in.at[part],
            device_id={"grp": partner},
            device_id_type=MESH,
        )

    def table_copy(step):
        return pltpu.make_async_remote_copy(
            src_ref=table_ref,
            dst_ref=tables.at[group],
            send_sem=table_out.at[step],
            recv_sem=table_in.at[step],
            device_id={"grp": lax.rem(group + step, groups)},
            device_id_type=MESH,
        )

    def start_table(step, none):
        table_copy(step).start()
        return none

    def wait_table(step, none):
        table_copy(step).wait()
        return none

    def page_copy(step, part):
        down, along = step // side, step % side
        target = (
            lax.rem(chip // side + down, side) * side + lax.rem(lax.rem(chip, side) + along, side)
        )
        return pltpu.make_async_remote_copy(
            src_ref=ordered.at[target, *place_of(part)],
            dst_ref=arrived.at[chip, *place_of(part)],
            send_sem=page_out.at[step, part],
            recv_sem=page_in.at[step, part],
            device_id={"grp": target * 2 + core},
            device_id_type=MESH,
        )

    def request_of(owner, entry):
        return tables_here[2 * owner + entry // page_count, 0, entry % page_count]

    def first_of(owner, request, value):
        found = 0
        for entry in reversed(range(2 * page_count)):
            found = jnp.where(request_of(owner, entry) == request, value(entry), found)
        return found

    own_start(0)
    for part in range(parts):
        half_copy(part).start()
    lax.fori_loop(1, groups, start_table, 0)
    relay(0)
    own_start(1)
    own_start(2)
    table_own.wait()
    lax.fori_loop(1, groups, wait_table, 0)
    save = pltpu.make_async_copy(tables, tables_here, table_save)
    save.start()
    save.wait()

    def pick(request, none):
        picks[request] = first_of(chip, request, lambda entry: entry)
        return none

    lax.fori_loop(0, chips, pick, 0)

    def send_pieces(part):
        for step in PAGE_ORDER:
            page_copy(step, part).start()

    for part in range(parts):
        piece_load(part).wait()
        half_copy(part).wait_recv()
        layer, lines = place_of(part)

        def order_piece(request, none):
            ordered[request, layer, lines] = pages[part][picks[request]]
            return none

        lax.fori_loop(0, chips, order_piece, 0)
        if part:
            send_pieces(part - 1)
    send_pieces(parts - 1)
    stay = pltpu.make_async_copy(ordered.at[chip], arrived.at[chip], place_out)
    stay.start()
    for load in loads:
        load.wait()

    def slot_from(owner, none):
        slots[owner] = first_of(
            owner,
            chip,
            lambda entry: tables_here[2 * owner + entry // page_count, 1, entry % page_count],
        )
        return none

    lax.fori_loop(0, chips, slot_from, 0)

    for request in range(chips):
        powers[request] = 1 << request

    def repeats(owner, twice):
        total = 0
        for entry in range(2 * page_count):
            total += powers[request_of(owner, entry)]
        return jnp.where(total == (1 << chips) - 1, twice, 1)

    twice_ref[0] = lax.fori_loop(0, chips, repeats, 0)

    length = length_ref[lax.axis_index("grp")]

    def finish(chunk):
        rows = rows_of(chunk)
        total = mix[rows, :]
        for step in sides:
            for side in sides:
                near_copy(chunk, step, side).wait_recv()
            total += got[step, rows, :].astype(jnp.float32)
        mixed_ref[rows, :] = total.astype(jnp.bfloat16)

    def visit(chunk, none):
        @pl.when(chunk + 1 < chunks)
        def _():
            relay(chunk + 1)

        for later in range(3, chunks):

            @pl.when(chunk == later - 3)
            def _():
                own_start(later)

        rows = rows_of(chunk)
        for step in sides:
            own_copy(chunk, step, 4 - step).wait_recv()
            relay_copy(chunk, step).wait_recv()
        sums = jnp.zeros((ROWS, 1), jnp.float32)
        squares = jnp.zeros((ROWS, 1), jnp.float32)
        for peer in range(tp):
            piece = whole[peer, rows, :].astype(jnp.float32)
            sums += jnp.sum(piece, axis=1, keepdims=True)
            squares += jnp.sum(piece * piece, axis=1, keepdims=True)
        center = sums * (1.0 / features)
        spread = squares * (1.0 / features) - center * center
        scale = lax.rsqrt(spread + EPS)
        for peer in range(tp):
            columns = pl.ds(peer * width, width)
            piece = whole[peer, rows, :].astype(jnp.float32)
            normed[:, columns] = (
                (piece - center) * scale * gain_ref[:, columns] + bias_ref[:, columns]
            ).astype(jnp.bfloat16)
        for part in range(3):
            columns = pl.ds(part * part_width, part_width)
            projected = (
                jnp.dot(normed[...], w_qkv[:, columns], preferred_element_type=jnp.float32)
                + b_qkv_ref[columns][None, :]
            )
            if part == 0:
                projected = projected * size ** (-0.5)
            qkv[rows, columns] = projected.astype(jnp.bfloat16)

        def head(number, none):
            def lanes(start):
                return pl.ds(pl.multiple_of(start, size), size)

            heads = [number * TOGETHER + other for other in range(TOGETHER)]
            queries = [qkv[rows, lanes(at * size)] for at in heads]

            def new_block(states, other, allowed):
                scores = [
                    score(query, qkv[rows_of(other), lanes(part_width + at * size)], allowed)
                    for query, at in zip(queries, heads)
                ]
                return tuple(
                    update(state, each, qkv[rows_of(other), lanes(2 * part_width + at * size)])
                    for state, each, at in zip(states, scores, heads)
                )

            states = (None,) * TOGETHER
            for block in range(prefix // WIDE):
                base = pl.ds(block * WIDE, WIDE)
                position = block * WIDE + lax.broadcasted_iota(jnp.int32, (1, WIDE), 1)
                scores = [
                    score(query, cache[base, lanes(at * 2 * size)], position < length)
                    for query, at in zip(queries, heads)
                ]
                states = tuple(
                    update(state, each, cache[base, lanes(at * 2 * size + size)])
                    for state, each, at in zip(states, scores, heads)
                )
            states = lax.fori_loop(
                0, chunk, lambda other, states: new_block(states, other, None), states
            )
            causal = lax.broadcasted_iota(jnp.int32, (ROWS, ROWS), 1) <= lax.broadcasted_iota(
                jnp.int32, (ROWS, ROWS), 0
            )
            states = new_block(states, chunk, causal)
            for (highest, totals, running), at in zip(states, heads):
                attended[:, lanes(at * size)] = (running / totals).astype(jnp.bfloat16)
            return none

        lax.fori_loop(0, head_count // TOGETHER, head, 0)

        @pl.when(chunk > 0)
        def _():
            pass_on(chunk - 1)

        @pl.when(chunk > 1)
        def _():
            finish(chunk - 2)

        def term(step):
            columns = pl.ds(pl.multiple_of(lax.rem(me + step, tp) * width, width), width)
            return jnp.dot(attended[...], w_out[:, columns], preferred_element_type=jnp.float32)

        terms[2, rows, :] = term(2).astype(jnp.bfloat16)
        for step in sides:
            far_copy(chunk, step).start()
        for step in sides:
            terms[step, rows, :] = term(step).astype(jnp.bfloat16)
            near_copy(chunk, step, 4 - step).start()
        mix[rows, :] = term(0) + whole[me, rows, :].astype(jnp.float32) + b_out_ref[...]

        return none

    lax.fori_loop(0, chunks, visit, 0)
    finish(chunks - 2)
    pass_on(chunks - 1)
    finish(chunks - 1)
    for chunk in range(chunks):
        for step in sides:
            for side in sides:
                own_copy(chunk, step, side).wait_send()
                near_copy(chunk, step, side).wait_send()
            relay_copy(chunk, step).wait_send()
            far_copy(chunk, step).wait_send()

    for part in range(parts):
        half_copy(part).wait_send()
        for step in PAGE_ORDER:
            page_copy(step, part).wait()

    stay.wait()


def block(
    tokens, ln_gain, ln_bias, w_qkv, b_qkv, w_out, b_out, kv_cache, prefix_len, kv_pages, page_table
):
    tp = lax.axis_size("tp")
    groups = lax.axis_size("grp")
    page_count, layers, page_len, page_width = kv_pages.shape
    held = (groups // 2, layers, page_len, page_width // 2)
    rows, width = tokens.shape
    head_count = HEADS // tp
    chunks = rows // ROWS
    bf16 = jnp.bfloat16
    return pl.pallas_call(
        functools.partial(block_kernel, tp, groups, head_count),
        name="block",
        out_shape=(
            jax.ShapeDtypeStruct((rows, width), bf16),
            jax.ShapeDtypeStruct(held, bf16),
            jax.ShapeDtypeStruct((groups // 2,), jnp.int32),
            jax.ShapeDtypeStruct((1,), jnp.int32),
        ),
        in_specs=[ANY, VMEM, VMEM, ANY, VMEM, ANY, VMEM, ANY, SMEM, ANY, ANY],
        out_specs=(VMEM, ANY, SMEM, SMEM),
        scratch_shapes=[
            pltpu.VMEM((tp, rows, width), bf16),
            pltpu.VMEM(w_qkv.shape, bf16),
            pltpu.VMEM(w_out.shape, bf16),
            pltpu.VMEM(kv_cache.shape, bf16),
            pltpu.VMEM((ROWS, tp * width), bf16),
            pltpu.VMEM((rows, w_qkv.shape[1]), bf16),
            pltpu.VMEM((ROWS, w_out.shape[0]), bf16),
            pltpu.VMEM((tp, rows, width), bf16),
            pltpu.VMEM((tp, rows, width), bf16),
            pltpu.VMEM((rows, width), jnp.float32),
            pltpu.SemaphoreType.DMA((4,)),
        ]
        + [pltpu.SemaphoreType.DMA((chunks, tp + 2))] * 8
        + [
            pltpu.VMEM(held, bf16),
            pltpu.VMEM((groups, 2, page_count), jnp.int32),
            pltpu.SMEM((groups, 2, page_count), jnp.int32),
            pltpu.SMEM((groups // 2,), jnp.int32),
            pltpu.SMEM((groups // 2,), jnp.int32),
            pltpu.SemaphoreType.DMA((PARTS,)),
            pltpu.SemaphoreType.DMA((PARTS,)),
            pltpu.SemaphoreType.DMA((PARTS,)),
            pltpu.SemaphoreType.DMA,
            pltpu.SemaphoreType.DMA((groups,)),
            pltpu.SemaphoreType.DMA((groups,)),
            pltpu.SemaphoreType.DMA,
            pltpu.SemaphoreType.DMA((groups // 2, PARTS)),
            pltpu.SemaphoreType.DMA((groups // 2, PARTS)),
            pltpu.SemaphoreType.DMA,
        ]
        + [pltpu.VMEM((held[0], layers * page_len // PARTS, held[3]), bf16)] * PARTS,
        cost_estimate=pl.CostEstimate(
            flops=40_000_000_000, bytes_accessed=20_000_000, transcendentals=0
        ),
        compiler_params=pltpu.CompilerParams(
            collective_id=0, has_side_effects=True, vmem_limit_bytes=63 << 20
        ),
    )(
        tokens,
        ln_gain[None],
        ln_bias[None],
        w_qkv,
        b_qkv,
        w_out,
        b_out[None],
        kv_cache,
        prefix_len,
        page_table.T,
        kv_pages,
    )


def shards(
    tokens, ln_gain, ln_bias, w_qkv, b_qkv, w_out, b_out, kv_cache, prefix_len, kv_pages, page_table
):
    mixed, arrived, slots, twice = block(
        tokens,
        ln_gain,
        ln_bias,
        w_qkv,
        b_qkv,
        w_out,
        b_out,
        kv_cache,
        prefix_len,
        kv_pages,
        page_table,
    )
    decode_pages, mixed = lax.cond(
        twice[0] > 0,
        lambda *once: (move_twice(kv_pages, page_table), keep_rows(once[2])),
        place_once,
        slots,
        arrived,
        mixed,
    )
    return (mixed, decode_pages)


def solution(mesh):
    placed = (
        P("grp", "tp"),
        P(),
        P(),
        P(None, "tp"),
        P("tp"),
        P("tp", None),
        P("tp"),
        P("grp", "tp"),
        P(),
        P("grp", None, None, "tp"),
        P("grp", None),
    )
    return jax.shard_map(
        shards,
        mesh=mesh,
        in_specs=placed,
        out_specs=(P("grp", "tp"), P("grp", None, None, None, "tp")),
        check_vma=False,
    )
```
